512 devices in a mesh: lat: 16 (over x_hi, y, core), lon: 32 (over z, x_lo).
Axes of the slice: x: 4 (x_hi: 2, x_lo: 2; x = x_hi * 2 + x_lo), y: 4, z: 16, core: 2. Of those that a mesh axis runs over, the one named last changes fastest.
Arguments:
- sample_field: float32 [32, 128, 64, 256], P('lat', 'lon'), may hold values from -6 to 6
- langevin_noise: bfloat16 [2, 32, 128, 64, 256], P(None, 'lat', 'lon'), may hold values from -6 to 6
- precision: bfloat16 [32, 128, 9, 64, 64], P('lat', 'lon'), as said below
- pattern: int32 [32, 128, 9], P('lat', 'lon'), may hold values from 0 to 8, as said below
- foot_weight: bfloat16 [32, 128, 64, 4, 64], P('lat', 'lon'), may hold values from -0.375 to 0.375
- foot_columns: int32 [32, 128, 64, 4], P('lat', 'lon'), may hold values from 0 to 8, as said below
- foot_count: int32 [32, 128, 64], P('lat', 'lon'), may hold values from 0 to 4, as said below
- observed: float32 [32, 128, 64], P('lat', 'lon'), may hold values from -6 to 6
- inverse_var: float32 [32, 128, 64], P('lat', 'lon'), may hold values from 0.5 to 4
Outputs:
- new_field: float32 [32, 128, 64, 256], P('lat', 'lon')
The draws below stay inside these ranges and needn't reach their ends.
Inputs may be any that keep to these rules, and one draw needn't show every extreme that they name: `pattern`: each block's nine slots name the nine offset codes, each once. `foot_columns`: the 4 codes of one footprint are distinct. `foot_count`: in every block the slots with nonzero count come first, and all blocks of one device have the same number of them, between 8 and 64; some device has all 64 in every block. Each block row's precision block in the slot of code 4 has a large diagonal.
All inputs are finite; a program needn't handle non-finite values.
Results may differ from the reference program's by a relative error of at most 0.0023.
Values may be sent and summed in bfloat16 or wider, within the bound.
No kernel may reach another device: no remote copies, remote signals or barrier semaphores. Data moves between devices by JAX's collectives and lax.ppermute only.
A program may use at most 64 MiB of HBM per device.

```python
import math
import jax
import jax.numpy as jnp
from jax import lax

CB = 64
NBF = 4
STEPS = 2
BLAT = 2
BLON = 4
CHAINS = 256
FPB = 64
NLAT = 32
NLON = 128


def offset_order(key, leading):
    scores = jax.random.randint(key, leading + (9,), 0, 1 << 20) * 16 + jnp.arange(9, dtype=jnp.int32)
    return jnp.argsort(scores, axis=-1).astype(jnp.int32)


def draw_pattern(key, part):
    return offset_order(jax.random.fold_in(key, 11), (NLAT, NLON))


def draw_precision(key, part):
    offsets = offset_order(jax.random.fold_in(key, 11), (NLAT, NLON))
    noise_key = jax.random.fold_in(key, 12)
    dims_full = (NLAT, NLON, 9, CB, CB)
    entries = jax.random.normal(noise_key, dims_full, jnp.float32)
    identity = jnp.eye(CB, dtype=jnp.float32)
    centre = (offsets == 4).astype(jnp.float32)[..., None, None]
    return (0.5 * entries / math.sqrt(CB) + 2.0 * centre * identity).astype(jnp.bfloat16)


def draw_foot_columns(key, part):
    offsets = offset_order(jax.random.fold_in(key, 21), (NLAT, NLON, FPB))
    return offsets[..., :NBF]


def draw_foot_count(key, part):
    levels = jax.random.randint(jax.random.fold_in(key, 31), (NLAT // BLAT, NLON // BLON), 0, 4)
    occupied_count = jnp.right_shift(jnp.full(levels.shape, FPB, jnp.int32), levels)
    fullest = jax.random.randint(jax.random.fold_in(key, 32), (), 0, levels.size)
    flat_index = jnp.arange(levels.size, dtype=jnp.int32).reshape(levels.shape)
    occupied_count = jnp.where(flat_index == fullest, FPB, occupied_count)
    occupied_count = jnp.repeat(jnp.repeat(occupied_count, BLAT, axis=0), BLON, axis=1)
    lengths = jax.random.randint(jax.random.fold_in(key, 33), (NLAT, NLON, FPB), 1, NBF + 1)
    slot_index = jnp.arange(FPB, dtype=jnp.int32)
    lengths = jnp.where(slot_index == 0, NBF, lengths)
    return jnp.where(slot_index < occupied_count[..., None], lengths, 0).astype(jnp.int32)


def level_of(rng, shape, pieces, least, high):
    loudness, own = 1.0, jax.random.fold_in(rng, 6)
    for position, parts in pieces:
        steps = jnp.exp(jax.random.uniform(jax.random.fold_in(own, position), (parts,), jnp.float32, least / len(pieces), high / len(pieces)))
        loudness = loudness * jnp.repeat(steps, shape[position] // parts).reshape([-1 if axis == position else 1 for axis in range(len(shape))])
    return loudness


def bell_draw(rng, shape, width, most, split=(), kind=jnp.bfloat16):
    drawn = width * jax.random.normal(rng, shape, jnp.float32)
    if split:
        drawn = drawn * level_of(rng, shape, split, -0.22, 0.18)
    return jnp.clip(drawn, -most, most).astype(kind)


def setup_inputs(seed: int = 0) -> dict:
    key_list = jax.random.split(jax.random.key(seed), 10)
    sample_field = bell_draw(key_list[0], (NLAT, NLON, CB, CHAINS), 1.0, 6.0, ((0, 16), (1, 32)), jnp.float32)
    langevin_noise = bell_draw(key_list[1], (STEPS, NLAT, NLON, CB, CHAINS), 1.0, 6.0, ((1, 16), (2, 32)))
    precision = draw_precision(jax.random.fold_in(key_list[9], 71), 0)
    pattern = draw_pattern(jax.random.fold_in(key_list[9], 71), 0)
    foot_weight = bell_draw(key_list[4], (NLAT, NLON, FPB, NBF, CB), (NBF * CB) ** -0.5, 0.375, ((0, 16), (1, 32)))
    foot_columns = draw_foot_columns(jax.random.fold_in(key_list[9], 71), 0)
    foot_count = draw_foot_count(jax.random.fold_in(key_list[9], 71), 0)
    observed = bell_draw(key_list[7], (NLAT, NLON, FPB), 1.0, 6.0, ((0, 16), (1, 32)), jnp.float32)
    inverse_var = jnp.clip(jnp.exp(math.log(4.0) - 2.0794415 * jax.random.uniform(key_list[8], (NLAT, NLON, FPB), jnp.float32) ** level_of(key_list[8], (NLAT, NLON, FPB), ((0, 16), (1, 32)), -0.2, 0.2)), 0.5, 4.0)
    return {"sample_field": sample_field, "langevin_noise": langevin_noise, "precision": precision, "pattern": pattern, "foot_weight": foot_weight, "foot_columns": foot_columns, "foot_count": foot_count, "observed": observed, "inverse_var": inverse_var}


step_size = 0.2

def pad_global(compact):
    blank_rows = jnp.zeros((1,) + compact.shape[1:], compact.dtype)
    extended = jnp.concatenate([blank_rows, compact, blank_rows], axis=0)
    return jnp.concatenate([extended[:, -1:], extended, extended[:, :1]], axis=1)

def reference(sample_field, langevin_noise, precision, pattern, foot_weight, foot_columns, foot_count, observed, inverse_var):
    sample = sample_field
    for update in range(STEPS):
        padded = pad_global(sample.astype(jnp.bfloat16))

        def visit_row(adjoint_pad, row):
            row = row.astype(jnp.int32)
            anchor = jnp.zeros((), jnp.int32)
            window = lax.dynamic_slice(padded, (row, anchor, anchor, anchor), (3, NLON + 2, CB, CHAINS))
            shifted = jnp.stack([window[offset // 3, offset % 3:offset % 3 + NLON] for offset in range(9)])
            row_precision = lax.dynamic_index_in_dim(precision, row, 0, False)
            row_pattern = lax.dynamic_index_in_dim(pattern, row, 0, False)
            select = (row_pattern[..., None] == jnp.arange(9, dtype=jnp.int32)).astype(jnp.float32)
            ordered = jnp.einsum('bko,bkcd->bocd', select, row_precision.astype(jnp.float32)).astype(jnp.bfloat16)
            prior_row = jnp.einsum('bocd,obds->bcs', ordered.astype(jnp.float32), shifted.astype(jnp.float32))
            weights = lax.dynamic_index_in_dim(foot_weight, row, 0, False)
            columns = lax.dynamic_index_in_dim(foot_columns, row, 0, False)
            entries = lax.dynamic_index_in_dim(foot_count, row, 0, False)
            target = lax.dynamic_index_in_dim(observed, row, 0, False)
            scale = lax.dynamic_index_in_dim(inverse_var, row, 0, False)
            active = jnp.arange(NBF, dtype=jnp.int32) < entries[..., None]
            masked = jnp.where(active[..., None], weights, jnp.zeros_like(weights)).astype(jnp.float32)
            code_hot = (columns[..., None] == jnp.arange(9, dtype=jnp.int32)).astype(jnp.float32)
            foot_matrix = jnp.einsum('bfjo,bfjc->bfoc', code_hot, masked).astype(jnp.bfloat16).astype(jnp.float32)
            forward = jnp.einsum('bfoc,obcs->bfs', foot_matrix, shifted.astype(jnp.float32))
            residual = (scale[..., None] * (forward - target[..., None])).astype(jnp.bfloat16)
            spread = jnp.einsum('bfoc,bfs->obcs', foot_matrix, residual.astype(jnp.float32))
            local = jnp.zeros((3, NLON + 2, CB, CHAINS), jnp.float32)
            for offset in range(9):
                local = local.at[offset // 3, offset % 3:offset % 3 + NLON].add(spread[offset])
            earlier = lax.dynamic_slice(adjoint_pad, (row, anchor, anchor, anchor), local.shape)
            adjoint_pad = lax.dynamic_update_slice(adjoint_pad, earlier + local, (row, anchor, anchor, anchor))
            return (adjoint_pad, prior_row)
        start = jnp.zeros((NLAT + 2, NLON + 2, CB, CHAINS), jnp.float32)
        adjoint_pad, prior_all = lax.scan(visit_row, start, jnp.arange(NLAT, dtype=jnp.int32))
        bounded = adjoint_pad[1:-1]
        bounded = bounded.at[:, 1].add(bounded[:, -1]).at[:, -2].add(bounded[:, 0])
        gradient = prior_all + bounded[:, 1:-1]
        sample = sample - step_size * gradient + math.sqrt(2.0 * step_size) * langevin_noise[update].astype(jnp.float32)
    return sample
```

```python
import math

import jax
import jax.numpy as jnp
from jax import lax
from jax.experimental import pallas as pl
from jax.experimental.pallas import tpu as pltpu
from jax.sharding import PartitionSpec as P

STEPS = 2
step_size = 0.2
BF = jnp.bfloat16
F32 = jnp.float32
VM = pltpu.VMEM


def shift_lon(block, by):
    count = lax.axis_size("lon")
    return lax.ppermute(block, "lon", [(i, (i + by) % count) for i in range(count)])


def shift_lat(block, by):
    count = lax.axis_size("lat")
    return lax.ppermute(
        block, "lat", [(i, i + by) for i in range(count) if 0 <= i + by < count]
    )


def pieces(x):
    high = lax.reduce_precision(x, 8, 7)
    rest = x - high
    middle = lax.reduce_precision(rest, 8, 7)
    return [high, middle, rest - middle]


def prior_matrix_kernel(pattern_ref, precision_ref, lp_ref, slot_ref):
    for b in range(2):
        for j in range(4):
            for k in range(9):
                slot_ref[(b * 4 + j) * 9 + pattern_ref[b, j, k]] = k
    blank = jnp.zeros((64, 64), BF)
    for b in range(2):
        for p in range(2):
            for dr in range(3):
                for t in range(2):
                    j = 2 * p + t
                    parts = [
                        precision_ref[b, j, slot_ref[(b * 4 + j) * 9 + dr * 3 + o]]
                        for o in range(3)
                    ]
                    parts = [blank] * t + parts + [blank] * (1 - t)
                    lp_ref[b, p, dr, t * 64 : (t + 1) * 64, :] = jnp.concatenate(parts, axis=1)


def foot_matrix_kernel(fw_ref, mt_ref, lf_ref, la_ref, ov_ref):
    rowblock = lax.broadcasted_iota(jnp.int32, (256, 256), 0) // 64
    laneblock = lax.broadcasted_iota(jnp.int32, (256, 256), 1) // 64
    lane_owner = lax.broadcasted_iota(jnp.int32, (16, 256), 1) // 64
    for i in range(4):
        meta = mt_ref[i].astype(F32)
        columns = jnp.transpose(meta, (1, 0))
        obs = columns[:, 4:5] + columns[:, 5:6] + columns[:, 6:7]
        ivar = columns[:, 7:8] + columns[:, 8:9] + columns[:, 9:10]
        ov_ref[0, i] = jnp.broadcast_to(obs, (384, 128))
        ov_ref[1, i] = jnp.broadcast_to(ivar, (384, 128))
        weights = fw_ref[i]
        for q in range(2):
            rows = slice(q * 128, q * 128 + 256)
            for dr in range(3):
                col = laneblock - rowblock + 2 * q
                need = jnp.where((col >= 0) & (col <= 2), col + 3 * dr, 99).astype(F32)
                total = jnp.zeros((256, 256), F32)
                for j in range(4):
                    one = weights[rows, j * 64 : (j + 1) * 64].astype(F32)
                    four = jnp.concatenate([one] * 4, axis=1)
                    total = total + jnp.where(columns[rows, j : j + 1] == need, four, 0.0)
                lf_ref[i, q, dr] = total.astype(BF)
        turned = jnp.transpose(weights.astype(F32), (1, 0))
        for b in range(2):
            if not 0 <= b - i + 2 <= 2:
                continue
            for p in range(2):
                lanes = slice(p * 128, p * 128 + 256)
                for t in range(2):
                    col = t - lane_owner[0:1] + 2
                    need = jnp.where((col >= 0) & (col <= 2), col + 3 * (b - i + 2), 99)
                    need = need.astype(F32)
                    total = jnp.zeros((64, 256), F32)
                    for j in range(4):
                        hit = (meta[j : j + 1, lanes] == need).astype(F32)
                        total = total + turned[j * 64 : (j + 1) * 64, lanes] * hit
                    la_ref[b, p, i - b, t * 64 : (t + 1) * 64, :] = total.astype(BF)


def dot(a, b):
    return jnp.dot(a, b, preferred_element_type=F32)


def step_kernel(last, x_ref, lf_ref, la_ref, lp_ref, ov_ref, sample_ref, noise_ref, *refs):
    out_ref = refs[0]
    res_ref = refs[-1]
    for i in range(4):
        half = []
        for q in range(2):
            acc = dot(lf_ref[i, q, 0], x_ref[i, q * 256 : (q + 1) * 256, :])
            for dr in (1, 2):
                acc = acc + dot(lf_ref[i, q, dr], x_ref[i + dr, q * 256 : (q + 1) * 256, :])
            half.append(acc)
        for part in range(3):
            rows = slice(part * 128, (part + 1) * 128)
            if part == 0:
                fwd = half[0][:128]
            elif part == 1:
                fwd = half[0][128:] + half[1][:128]
            else:
                fwd = half[1][128:]
            obs = ov_ref[0, i, rows, :]
            ivar = ov_ref[1, i, rows, :]
            for h in range(2):
                lanes = slice(h * 128, (h + 1) * 128)
                res_ref[i, rows, lanes] = (ivar * (fwd[:, lanes] - obs)).astype(BF)
    for b in range(2):
        for p in range(2):
            acc = None
            for dr in range(3):
                term = dot(lp_ref[b, p, dr], x_ref[b + 1 + dr, (1 + 2 * p) * 64 : (5 + 2 * p) * 64, :])
                acc = term if acc is None else acc + term
                acc = acc + dot(la_ref[b, p, dr], res_ref[b + dr, p * 128 : p * 128 + 256, :])
            rows = slice(p * 128, (p + 1) * 128)
            value = (
                sample_ref[b, rows, :]
                - step_size * acc
                + math.sqrt(2.0 * step_size) * noise_ref[b, rows, :].astype(F32)
            )
            out_ref[b, rows, :] = value
            if not last:
                refs[1][b, rows, :] = value.astype(BF)


def whole(n):
    return [pl.BlockSpec(memory_space=VM)] * n


PARAMS = pltpu.CompilerParams(vmem_limit_bytes=48 * 1024 * 1024)


def prior_matrix(pattern, precision):
    return pl.pallas_call(
        prior_matrix_kernel,
        out_shape=jax.ShapeDtypeStruct((2, 2, 3, 128, 256), BF),
        in_specs=[pl.BlockSpec(memory_space=pltpu.SMEM)] + whole(1),
        out_specs=whole(1)[0],
        scratch_shapes=[pltpu.SMEM((72,), jnp.int32)],
        compiler_params=PARAMS,
        cost_estimate=pl.CostEstimate(flops=2000000, bytes_accessed=3000000, transcendentals=0),
    )(pattern, precision)


def foot_matrix(fw, mt):
    return pl.pallas_call(
        foot_matrix_kernel,
        out_shape=(
            jax.ShapeDtypeStruct((4, 2, 3, 256, 256), BF),
            jax.ShapeDtypeStruct((2, 2, 3, 128, 256), BF),
            jax.ShapeDtypeStruct((2, 4, 384, 128), F32),
        ),
        in_specs=whole(2),
        out_specs=tuple(whole(3)),
        compiler_params=PARAMS,
        cost_estimate=pl.CostEstimate(flops=20000000, bytes_accessed=6000000, transcendentals=0),
    )(fw, mt)


def step(window, lf, la, lp, ov, sample, noise, last):
    shapes = [jax.ShapeDtypeStruct((2, 256, 256), F32)]
    if not last:
        shapes.append(jax.ShapeDtypeStruct((2, 256, 256), BF))
    return pl.pallas_call(
        lambda *refs: step_kernel(last, *refs),
        name="langevin_last" if last else "langevin_first",
        out_shape=tuple(shapes),
        in_specs=whole(7),
        out_specs=tuple(whole(len(shapes))),
        scratch_shapes=[pltpu.VMEM((4, 384, 256), BF)],
        compiler_params=PARAMS,
        cost_estimate=pl.CostEstimate(flops=1200000000, bytes_accessed=9000000, transcendentals=0),
    )(window, lf, la, lp, ov, sample, noise)


def local(
    sample_field,
    langevin_noise,
    precision,
    pattern,
    foot_weight,
    foot_columns,
    foot_count,
    observed,
    inverse_var,
):
    sample = sample_field.reshape(2, 256, 256)
    noise = langevin_noise.reshape(STEPS, 2, 256, 256)
    compact = sample.astype(BF)
    active = jnp.arange(4, dtype=jnp.int32) < foot_count[..., None]
    fw = jnp.where(active[..., None], foot_weight, jnp.zeros_like(foot_weight))
    fw = fw.reshape(2, 256, 256)
    rows = [foot_columns.transpose(0, 3, 1, 2).reshape(2, 4, 256).astype(F32)]
    rows += [part.reshape(2, 1, 256) for part in pieces(observed) + pieces(inverse_var)]
    rows.append(jnp.zeros((2, 6, 256), F32))
    mt = jnp.concatenate(rows, axis=1).astype(BF)

    def edge(cells, col):
        meta = jnp.pad(mt[:, :, col * 64 : (col + 1) * 64], ((0, 0), (0, 0), (0, 192)))
        return jnp.concatenate([compact[:, cells], fw[:, col * 64 : (col + 1) * 64], meta], axis=1)

    lp = prior_matrix(pattern, precision)
    west = shift_lon(edge(slice(128, 256), 3), 1)
    east = shift_lon(edge(slice(0, 128), 0), -1)
    middle = jnp.concatenate([west[:, :128], compact, east[:, :128]], axis=1)
    fw = jnp.concatenate([west[:, 128:192], fw, east[:, 128:192]], axis=1)
    mt = jnp.concatenate([west[:, 192:, :64], mt, east[:, 192:, :64]], axis=2)
    flat = middle.reshape(1024, 256)

    def band(row):
        meta = jnp.pad(mt[row], ((0, 0), (0, 128)))
        return jnp.concatenate([flat, fw[row], meta[:, :256], meta[:, 256:]], axis=0)

    north = shift_lat(band(1), 1)
    south = shift_lat(band(0), -1)

    def unband(got):
        meta = jnp.concatenate([got[1408:1424], got[1424:1440, :128]], axis=1)
        return got[:1024].reshape(2, 512, 256), got[1024:1408][None], meta[None]

    (xn, fn, mn), (xs, fs, ms) = unband(north), unband(south)
    window = jnp.concatenate([xn, middle, xs], axis=0)
    fw = jnp.concatenate([fn, fw, fs], axis=0)
    mt = jnp.concatenate([mn, mt, ms], axis=0)
    lf, la, ov = foot_matrix(fw, mt)
    sample, compact = step(window, lf, la, lp, ov, sample, noise[0], False)

    west = shift_lon(compact[:, 128:], 1)
    east = shift_lon(compact[:, :128], -1)
    middle = jnp.concatenate([west, compact, east], axis=1)
    window = jnp.concatenate([shift_lat(middle, 1), middle, shift_lat(middle, -1)], axis=0)
    (sample,) = step(window, lf, la, lp, ov, sample, noise[1], True)
    return sample.reshape(sample_field.shape)


def solution(mesh):
    placed = (
        P("lat", "lon", None, None),
        P(None, "lat", "lon", None, None),
        P("lat", "lon", None, None, None),
        P("lat", "lon", None),
        P("lat", "lon", None, None, None),
        P("lat", "lon", None, None),
        P("lat", "lon", None),
        P("lat", "lon", None),
        P("lat", "lon", None),
    )
    return jax.shard_map(
        local, mesh=mesh, in_specs=placed, out_specs=P("lat", "lon", None, None), check_vma=False
    )
```

```python
import math

import jax
import jax.numpy as jnp
from jax import lax
from jax.experimental import pallas as pl
from jax.experimental.pallas import tpu as pltpu
from jax.sharding import PartitionSpec as P

STEPS = 2
step_size = 0.2
BF = jnp.bfloat16
F32 = jnp.float32
VM = pltpu.VMEM


def shift_lon(block, by):
    count = lax.axis_size("lon")
    return lax.ppermute(block, "lon", [(i, (i + by) % count) for i in range(count)])


def swap_lat(block, first):
    count = lax.axis_size("lat")
    pairs = [(i, i + 1) for i in range(first, count - 1, 2)]
    return lax.ppermute(block, "lat", pairs + [(b, a) for a, b in pairs])


def dot(a, b):
    return jnp.dot(a, b, preferred_element_type=F32)


def split(x):
    high = x.astype(BF)
    rest = x - high.astype(F32)
    middle = rest.astype(BF)
    return [high.astype(F32), middle.astype(F32), rest - middle.astype(F32)]


def prepare_kernel(sample_ref, columns_ref, count_ref, obs_ref, ivar_ref, compact_ref, mt_ref):
    compact_ref[...] = sample_ref[...].astype(BF)
    eye = (
        lax.broadcasted_iota(jnp.int32, (256, 256), 0)
        == lax.broadcasted_iota(jnp.int32, (256, 256), 1)
    ).astype(F32).astype(BF)
    slot = lax.broadcasted_iota(jnp.int32, (4, 256), 0)
    for b in range(2):
        codes = lax.dot_general(
            columns_ref[b].astype(F32).astype(BF), eye, (((0,), (0,)), ((), ())),
            preferred_element_type=F32,
        )

        def row(ref):
            return jnp.concatenate([ref[b, c : c + 1, :] for c in range(4)], axis=1)

        codes = jnp.where(slot < row(count_ref), codes, 99.0)
        rows = [codes] + split(row(obs_ref)) + split(row(ivar_ref)) + [jnp.zeros((6, 256), F32)]
        mt_ref[b] = jnp.concatenate(rows, axis=0).astype(BF)


def prior_matrix_kernel(pattern_ref, precision_ref, lp_ref, slot_ref):
    for b in range(2):
        for j in range(4):
            for k in range(9):
                slot_ref[(b * 4 + j) * 9 + pattern_ref[b, j, k]] = k
    blank = jnp.zeros((64, 64), BF)
    for b in range(2):
        for p in range(2):
            for dr in range(3):
                for t in range(2):
                    j = 2 * p + t
                    parts = [
                        precision_ref[b, j, slot_ref[(b * 4 + j) * 9 + dr * 3 + o]]
                        for o in range(3)
                    ]
                    parts = [blank] * t + parts + [blank] * (1 - t)
                    lp_ref[b, p, dr, t * 64 : (t + 1) * 64, :] = jnp.concatenate(parts, axis=1)


def lanes_iota(n):
    return lax.broadcasted_iota(jnp.int32, (1, n), 1) // 64


def build_forward(weights, columns, store):
    for oc in range(6):
        rows = slice(oc * 64, (oc + 1) * 64)
        pair, code = [], []
        for j in range(4):
            one = weights[rows, j * 64 : (j + 1) * 64]
            pair.append(jnp.concatenate([one, one], axis=1))
            code.append(jnp.broadcast_to(columns[rows, j : j + 1], (64, 128)))
        for q in range(2):
            local_oc = oc - 2 * q
            if not 0 <= local_oc < 4:
                continue
            for h in range(2):
                col = lanes_iota(128) + 2 * h - local_oc + 2 * q
                some = any(0 <= 2 * h + x - local_oc + 2 * q <= 2 for x in range(2))
                for dr in range(3):
                    total = jnp.zeros((64, 128), F32)
                    if some:
                        need = jnp.where((col >= 0) & (col <= 2), col + 3 * dr, 77).astype(F32)
                        for j in range(4):
                            total = jnp.where(code[j] == need, pair[j], total)
                    store(q, dr, slice(local_oc * 64, local_oc * 64 + 64), slice(h * 128, h * 128 + 128), total.astype(BF))


def build_adjoint(turned, meta, b, i, store):
    for p in range(2):
        lanes = slice(p * 128, p * 128 + 256)
        for t in range(2):
            col = t - lanes_iota(256) + 2
            need = jnp.where((col >= 0) & (col <= 2), col + 3 * (b - i + 2), 77).astype(F32)
            total = jnp.zeros((64, 256), F32)
            for j in range(4):
                hit = meta[j : j + 1, lanes] == need
                total = jnp.where(hit, turned[j * 64 : (j + 1) * 64, lanes], total)
            store(p, slice(t * 64, t * 64 + 64), total.astype(BF))


def scales(columns):
    obs = columns[:, 4:5] + columns[:, 5:6] + columns[:, 6:7]
    ivar = columns[:, 7:8] + columns[:, 8:9] + columns[:, 9:10]
    return obs, ivar


def forward_into(acc_ref, i, lf, x, fresh):
    for q in range(2):
        term = dot(lf(q), x[q * 256 : (q + 1) * 256, :])
        lo = slice(q * 128, q * 128 + 128)
        hi = slice(q * 128 + 128, q * 128 + 256)
        if fresh and q == 0:
            acc_ref[i, 0:256, :] = term
        elif fresh:
            acc_ref[i, lo, :] += term[:128]
            acc_ref[i, hi, :] = term[128:]
        else:
            acc_ref[i, q * 128 : q * 128 + 256, :] += term


def prior_into(grad_ref, b, dr, lp_ref, x, fresh):
    for p in range(2):
        term = dot(lp_ref[b, p, dr], x[(1 + 2 * p) * 64 : (5 + 2 * p) * 64, :])
        rows = slice(p * 128, p * 128 + 128)
        if fresh:
            grad_ref[b, rows, :] = term
        else:
            grad_ref[b, rows, :] += term


def middle_terms(first, x_ref, lp_ref, lfm_ref, lfo_ref, acc_ref, grad_ref):
    for i, dr, r in ((1, 1, 0), (1, 2, 1), (2, 0, 0), (2, 1, 1)):
        forward_into(
            acc_ref, i, lambda q: lfm_ref[i - 1, q, dr], x_ref[r], (i, dr) in ((1, 1), (2, 0))
        )
    if not first:
        forward_into(acc_ref, 0, lambda q: lfo_ref[0, q, 2], x_ref[0], True)
        forward_into(acc_ref, 3, lambda q: lfo_ref[1, q, 0], x_ref[1], True)
    for b, dr, r in ((0, 1, 0), (0, 2, 1), (1, 0, 0), (1, 1, 1)):
        prior_into(grad_ref, b, dr, lp_ref, x_ref[r], (b, dr) in ((0, 1), (1, 0)))


def middle_first_kernel(x_ref, fw_ref, mt_ref, lp_ref, lfm_ref, lam_ref, acc_ref, grad_ref):
    for k in range(2):
        i = k + 1
        meta = mt_ref[k].astype(F32)
        columns = jnp.transpose(meta, (1, 0))
        weights = fw_ref[k].astype(F32)

        def put(q, dr, rows, lanes, value):
            lfm_ref[k, q, dr, rows, lanes] = value

        build_forward(weights, columns, put)
        turned = jnp.transpose(weights, (1, 0))
        for b in range(2):

            def put_adjoint(p, rows, value):
                lam_ref[k, b, p, rows, :] = value

            build_adjoint(turned, meta, b, i, put_adjoint)
    middle_terms(True, x_ref, lp_ref, lfm_ref, None, acc_ref, grad_ref)


def middle_last_kernel(x_ref, lp_ref, lfm_ref, lfo_ref, acc_ref, grad_ref):
    middle_terms(False, x_ref, lp_ref, lfm_ref, lfo_ref, acc_ref, grad_ref)


def finish_kernel(first, *refs):
    (side_ref, x_ref, far_ref, pair_ref, halo_ref, mtm_ref, lp_ref, lfm_ref, lam_ref) = refs[:9]
    if first:
        acc_in, grad_in, sample_ref, noise_ref = refs[9:13]
        out_ref, compact_ref, lfo_ref, lao_ref, mto_ref = refs[13:18]
        lines_ref, res_ref, acc_ref, grad_ref = refs[18:]
    else:
        lfo_ref, lao_ref, mto_ref, acc_in, grad_in, sample_ref, noise_ref = refs[9:16]
        out_ref = refs[16]
        lines_ref, res_ref, acc_ref, grad_ref = refs[17:]
    side = side_ref[0]
    for r in range(2):
        lines_ref[0, r] = far_ref[r * 512 : (r + 1) * 512, :]
        lines_ref[1, r, 0:128, :] = halo_ref[r * 256 : r * 256 + 128, :]
        lines_ref[1, r, 128:384, :] = pair_ref[1 - side, r]
        lines_ref[1, r, 384:512, :] = halo_ref[r * 256 + 128 : r * 256 + 256, :]

    acc_ref[1:3] = acc_in[1:3]
    if not first:
        acc_ref[0] = acc_in[0]
        acc_ref[3] = acc_in[3]
    grad_ref[...] = grad_in[...]

    def line(w):
        if w < 2:
            return lines_ref.at[side, w]
        if w < 4:
            return x_ref.at[w - 2]
        return lines_ref.at[1 - side, w - 4]

    if first:
        for k in range(2):
            i = 3 * k
            near = (side == 0) if k == 0 else (side == 1)

            foot = jnp.where(near, far_ref[1024:1440, :], halo_ref[512:928, :])
            weights = foot[0:384].astype(F32)
            meta = jnp.concatenate([foot[384:400], foot[400:416, :128]], axis=1).astype(F32)
            mto_ref[k] = meta.astype(BF)

            def put(q, dr, rows, lanes, value):
                lfo_ref[k, q, dr, rows, lanes] = value

            build_forward(weights, jnp.transpose(meta, (1, 0)), put)

            def put_adjoint(p, rows, value):
                lao_ref[k, p, rows, :] = value

            build_adjoint(jnp.transpose(weights, (1, 0)), meta, k, i, put_adjoint)

    for i in range(4):
        edge = i in (0, 3)
        for dr in range(3):
            w = i + dr
            if w in (2, 3) and not (first and edge):
                continue
            source = (lambda q: lfo_ref[i // 3, q, dr]) if edge else (lambda q: lfm_ref[i - 1, q, dr])
            forward_into(acc_ref, i, source, line(w), first and edge and dr == 0)
        meta = (mto_ref[i // 3] if edge else mtm_ref[i - 1]).astype(F32)
        obs, ivar = scales(jnp.transpose(meta, (1, 0)))
        res_ref[i] = (ivar * (acc_ref[i] - obs)).astype(BF)
    for b in range(2):
        dr = 0 if b == 0 else 2
        prior_into(grad_ref, b, dr, lp_ref, line(b + 1 + dr), False)
        for p in range(2):
            rows = slice(p * 128, (p + 1) * 128)
            acc = grad_ref[b, rows, :]
            for i in range(b, b + 3):
                left = lao_ref[i // 3, p] if i in (0, 3) else lam_ref[i - 1, b, p]
                acc = acc + dot(left, res_ref[i, p * 128 : p * 128 + 256, :])
            value = (
                sample_ref[b, rows, :]
                - step_size * acc
                + math.sqrt(2.0 * step_size) * noise_ref[b, rows, :].astype(F32)
            )
            out_ref[b, rows, :] = value
            if first:
                compact_ref[b, rows, :] = value.astype(BF)


def shape(dims, dtype=BF):
    return jax.ShapeDtypeStruct(dims, dtype)


def call(kernel, name, outs, args, scratch=(), scalars=0, flops=0, moved=0):
    spec = pl.BlockSpec(memory_space=VM)
    return pl.pallas_call(
        kernel,
        name=name,
        out_shape=tuple(outs),
        in_specs=[pl.BlockSpec(memory_space=pltpu.SMEM)] * scalars + [spec] * (len(args) - scalars),
        out_specs=tuple([spec] * len(outs)),
        scratch_shapes=list(scratch),
        compiler_params=pltpu.CompilerParams(vmem_limit_bytes=16 * 1024 * 1024),
        cost_estimate=pl.CostEstimate(flops=flops, bytes_accessed=moved, transcendentals=0),
    )(*args)


def finish(first, args):
    outs = [shape((2, 256, 256), F32)]
    if first:
        outs += [
            shape((2, 256, 256)),
            shape((2, 2, 3, 256, 256)),
            shape((2, 2, 128, 256)),
            shape((2, 16, 384)),
        ]
    return call(
        lambda *refs: finish_kernel(first, *refs),
        "finish_first" if first else "finish_last",
        outs,
        args,
        scratch=[
            pltpu.VMEM((2, 2, 512, 256), BF),
            pltpu.VMEM((4, 384, 256), BF),
            pltpu.VMEM((4, 384, 256), F32),
            pltpu.VMEM((2, 256, 256), F32),
        ],
        scalars=1,
        flops=800000000,
        moved=5000000,
    )


def local(
    sample_field,
    langevin_noise,
    precision,
    pattern,
    foot_weight,
    foot_columns,
    foot_count,
    observed,
    inverse_var,
):
    side = lax.axis_index("lat") % 2
    sides = jnp.full((1,), side, jnp.int32)
    sample = sample_field.reshape(2, 256, 256)
    noise = langevin_noise.reshape(STEPS, 2, 256, 256)
    fw = foot_weight.reshape(2, 256, 256)
    compact, mt = call(
        prepare_kernel,
        "prepare",
        [shape((2, 256, 256)), shape((2, 16, 256))],
        (sample, foot_columns.reshape(2, 256, 4), foot_count, observed, inverse_var),
        flops=1000000,
        moved=1000000,
    )

    def edge(cells, col):
        meta = jnp.pad(mt[:, :, col * 64 : (col + 1) * 64], ((0, 0), (0, 0), (0, 192)))
        return jnp.concatenate([compact[:, cells], fw[:, col * 64 : (col + 1) * 64], meta], axis=1)

    west = shift_lon(edge(slice(128, 256), 3), 1)
    (lp,) = call(
        prior_matrix_kernel,
        "prior_matrix",
        [shape((2, 2, 3, 128, 256))],
        (pattern, precision),
        scratch=[pltpu.SMEM((72,), jnp.int32)],
        scalars=1,
        flops=2000000,
        moved=3000000,
    )
    leaving, lp = lax.optimization_barrier((edge(slice(0, 128), 0), lp))
    east = shift_lon(leaving, -1)
    middle = jnp.concatenate([west[:, :128], compact, east[:, :128]], axis=1)
    fw = jnp.concatenate([west[:, 128:192], fw, east[:, 128:192]], axis=1)
    mt = jnp.concatenate([west[:, 192:, :64], mt, east[:, 192:, :64]], axis=2)

    def foot_row(row):
        meta = jnp.pad(mt[row], ((0, 0), (0, 128)))
        return jnp.concatenate([fw[row], meta[:, :256], meta[:, 256:]], axis=0)

    foot = jnp.stack([foot_row(0), foot_row(1)])
    far_foot = jnp.where(side == 0, foot[0], foot[1])
    mate_foot = jnp.where(side == 0, foot[1], foot[0])

    def lat_exchange(compact, middle, west, east, far_extra, mate_extra):
        far = swap_lat(jnp.concatenate([middle.reshape(1024, 256)] + far_extra, axis=0), 1)
        halo = jnp.concatenate([west, east], axis=1).reshape(512, 256)
        halo = swap_lat(jnp.concatenate([halo] + mate_extra, axis=0), 0)
        count = lax.axis_size("lat")
        pair = lax.all_gather(
            compact, "lat", axis_index_groups=[[i, i + 1] for i in range(0, count, 2)]
        )
        return far, pair, halo

    far, pair, halo = lat_exchange(
        compact, middle, west[:, :128], east[:, :128], [far_foot], [mate_foot]
    )
    lfm, lam, acc, grad = call(
        middle_first_kernel,
        "middle_first",
        [
            shape((2, 2, 3, 256, 256)),
            shape((2, 2, 2, 128, 256)),
            shape((4, 384, 256), F32),
            shape((2, 256, 256), F32),
        ],
        (middle, fw, mt, lp),
        flops=600000000,
        moved=20000000,
    )
    sample, compact, lfo, lao, mto = finish(
        True,
        (sides, middle, far, pair, halo, mt, lp, lfm, lam, acc, grad, sample, noise[0]),
    )

    west = shift_lon(compact[:, 128:], 1)
    east = shift_lon(compact[:, :128], -1)
    middle = jnp.concatenate([west, compact, east], axis=1)
    far, pair, halo = lat_exchange(compact, middle, west, east, [], [])
    acc, grad = call(
        middle_last_kernel,
        "middle_last",
        [shape((4, 384, 256), F32), shape((2, 256, 256), F32)],
        (middle, lp, lfm, lfo),
        flops=600000000,
        moved=20000000,
    )
    (sample,) = finish(
        False,
        (sides, middle, far, pair, halo, mt, lp, lfm, lam, lfo, lao, mto, acc, grad, sample, noise[1]),
    )
    return sample.reshape(sample_field.shape)


def solution(mesh):
    placed = (
        P("lat", "lon", None, None),
        P(None, "lat", "lon", None, None),
        P("lat", "lon", None, None, None),
        P("lat", "lon", None),
        P("lat", "lon", None, None, None),
        P("lat", "lon", None, None),
        P("lat", "lon", None),
        P("lat", "lon", None),
        P("lat", "lon", None),
    )
    return jax.shard_map(
        local, mesh=mesh, in_specs=placed, out_specs=P("lat", "lon", None, None), check_vma=False
    )
```

```python
import math

import jax
import jax.numpy as jnp
from jax import lax
from jax.experimental import pallas as pl
from jax.experimental.pallas import tpu as pltpu
from jax.sharding import PartitionSpec as P

STEPS = 2
step_size = 0.2
BF = jnp.bfloat16
F32 = jnp.float32
VM = pltpu.VMEM


def shift_lon(block, by):
    count = lax.axis_size("lon")
    return lax.ppermute(block, "lon", [(i, (i + by) % count) for i in range(count)])


def swap_lat(block, first):
    count = lax.axis_size("lat")
    pairs = [(i, i + 1) for i in range(first, count - 1, 2)]
    return lax.ppermute(block, "lat", pairs + [(b, a) for a, b in pairs])


def dot(a, b):
    return jnp.dot(a, b, preferred_element_type=F32)


def split(x):
    high = x.astype(BF)
    rest = x - high.astype(F32)
    middle = rest.astype(BF)
    return [high.astype(F32), middle.astype(F32), rest - middle.astype(F32)]


def prepare_kernel(sample_ref, stats_ref, fw_ref, compact_ref, mt_ref, west_ref, east_ref):
    slot = lax.broadcasted_iota(jnp.int32, (4, 256), 0).astype(F32)
    for b in range(2):
        stats = jnp.concatenate([stats_ref[b, c] for c in range(4)], axis=1)
        codes = jnp.where(slot < stats[4:5], stats[0:4], 99.0)
        rows = [codes] + split(stats[5:6]) + split(stats[6:7]) + [jnp.zeros((6, 256), F32)]
        meta = jnp.concatenate(rows, axis=0).astype(BF)
        mt_ref[b] = meta
        compact = sample_ref[b].astype(BF)
        compact_ref[b] = compact
        west_ref[b, 0:128, :] = compact[128:256]
        east_ref[b, 0:128, :] = compact[0:128]
        west_ref[b, 128:192, :] = fw_ref[b, 192:256, :]
        east_ref[b, 128:192, :] = fw_ref[b, 0:64, :]
        west_ref[b, 192:208, :] = jnp.concatenate([meta[:, 192:256]] * 4, axis=1)
        east_ref[b, 192:208, :] = meta


def prior_matrix_kernel(pattern_ref, precision_ref, lp_ref, slot_ref):
    for b in range(2):
        for j in range(4):
            for k in range(9):
                slot_ref[(b * 4 + j) * 9 + pattern_ref[b, j, k]] = k
    blank = jnp.zeros((64, 64), BF)
    for b in range(2):
        for p in range(2):
            for dr in range(3):
                for t in range(2):
                    j = 2 * p + t
                    parts = [
                        precision_ref[b, j, slot_ref[(b * 4 + j) * 9 + dr * 3 + o]]
                        for o in range(3)
                    ]
                    parts = [blank] * t + parts + [blank] * (1 - t)
                    lp_ref[b, p, dr, t * 64 : (t + 1) * 64, :] = jnp.concatenate(parts, axis=1)


def lanes_iota(n):
    return lax.broadcasted_iota(jnp.int32, (1, n), 1) // 64


def build_forward(weights, meta, store):
    codes = jnp.transpose(meta, (1, 0))
    for oc in range(6):
        rows = slice(oc * 64, (oc + 1) * 64)
        pair, code = [], []
        for j in range(4):
            one = weights[rows, j * 64 : (j + 1) * 64]
            pair.append(jnp.concatenate([one, one], axis=1).astype(KIND))
            code.append(jnp.broadcast_to(codes[rows, j : j + 1], (64, 128)).astype(KIND))
        for q in range(2):
            at = oc - 2 * q
            if not 0 <= at < 4:
                continue
            for h in range(2):
                shift = 2 * h - at + 2 * q
                col = lanes_iota(128) + shift
                some = any(0 <= shift + x <= 2 for x in range(2))
                for dr in range(3):
                    total = jnp.zeros((64, 128), KIND)
                    if some:
                        need = jnp.where((col >= 0) & (col <= 2), col + 3 * dr, 77)
                        need = jnp.broadcast_to(need.astype(F32), (64, 128)).astype(KIND)
                        for j in range(4):
                            total = jnp.where(code[j] == need, pair[j], total)
                    store(
                        q,
                        dr,
                        slice(at * 64, at * 64 + 64),
                        slice(h * 128, h * 128 + 128),
                        total.astype(BF),
                    )


def build_adjoint(turned, meta, code_row, store):
    for p in range(2):
        lanes = slice(p * 128, p * 128 + 256)
        for t in range(2):
            col = t - lanes_iota(256) + 2
            need = jnp.where((col >= 0) & (col <= 2), col + 3 * code_row, 77).astype(F32)
            total = jnp.zeros((64, 256), F32)
            for j in range(4):
                hit = meta[j : j + 1, lanes] == need
                total = jnp.where(hit, turned[j * 64 : (j + 1) * 64, lanes], total)
            store(p, slice(t * 64, t * 64 + 64), total.astype(BF))


def unpack_foot(foot_ref, at):
    weights = foot_ref[at : at + 384, :].astype(F32)
    meta = [foot_ref[at + 384 : at + 400, :], foot_ref[at + 400 : at + 416, :128]]
    return weights, jnp.concatenate(meta, axis=1).astype(F32)


def forward(terms):
    halves = []
    for q in range(2):
        total = None
        for operand, field in terms:
            term = dot(operand(q), field[q * 256 : (q + 1) * 256, :])
            total = term if total is None else total + term
        halves.append(total)
    low, high = halves
    return [low[:128], low[128:] + high[:128], high[128:]]


def residual(parts, meta, res_ref, slot):
    columns = jnp.transpose(meta, (1, 0))
    obs = columns[:, 4:5] + columns[:, 5:6] + columns[:, 6:7]
    ivar = columns[:, 7:8] + columns[:, 8:9] + columns[:, 9:10]
    for n in range(3):
        rows = slice(n * 128, (n + 1) * 128)
        res_ref[slot, rows, :] = (ivar[rows] * (parts[n] - obs[rows])).astype(BF)


def field_of(x, p):
    return x[(1 + 2 * p) * 64 : (5 + 2 * p) * 64, :]


def from_residual(res_ref, slot, p):
    return res_ref[slot, p * 128 : p * 128 + 256, :]


def middle_kernel(first, *refs):
    if first:
        side_ref, x_ref, fw_ref, mt_ref, pair_ref, halo_ref, lp_ref = refs[:7]
        lfm_ref, lam_ref, lft_ref, lat_ref, mtt_ref, part_ref, grad_ref = refs[7:14]
        mate_ref, res_ref = refs[14:]
    else:
        (side_ref, x_ref, mt_ref, pair_ref, halo_ref, lp_ref) = refs[:6]
        lfm_ref, lam_ref, lft_ref, lat_ref, mtt_ref, lff_ref = refs[6:12]
        part_ref, grad_ref = refs[12:14]
        mate_ref, res_ref = refs[14:]
    side = side_ref[0]
    for m in range(2):
        mate_ref[m, 0:128, :] = halo_ref[m * 256 : m * 256 + 128, :]
        mate_ref[m, 128:384, :] = pair_ref[1 - side, m]
        mate_ref[m, 384:512, :] = halo_ref[m * 256 + 128 : m * 256 + 256, :]
    if first:
        for k in range(2):
            meta = mt_ref[k].astype(F32)
            weights = fw_ref[k].astype(F32)

            def put(q, dr, rows, lanes, value):
                lfm_ref[k, q, dr, rows, lanes] = value

            build_forward(weights, meta, put)
            turned = jnp.transpose(weights, (1, 0))
            for b in range(2):

                def put_adjoint(p, rows, value):
                    lam_ref[k, b, p, rows, :] = value

                build_adjoint(turned, meta, b - k + 1, put_adjoint)
        weights, meta = unpack_foot(halo_ref, 512)
        mtt_ref[...] = meta.astype(BF)

        def put_mate(q, dr, rows, lanes, value):
            lft_ref[q, dr, rows, lanes] = value

        def put_mate_adjoint(p, rows, value):
            lat_ref[p, rows, :] = value

        build_forward(weights, meta, put_mate)
        build_adjoint(jnp.transpose(weights, (1, 0)), meta, 2 * side, put_mate_adjoint)

    parts = forward(
        [(lambda q, r=r: lfm_ref[1 - side, q, r + side], x_ref.at[r]) for r in range(2)]
        + [(lambda q: lfm_ref[1 - side, q, 2 - 2 * side], mate_ref.at[side])]
    )
    residual(parts, mt_ref[1 - side].astype(F32), res_ref, 0)
    parts = forward(
        [(lambda q, m=m: lft_ref[q, m + 1 - side], mate_ref.at[m]) for m in range(2)]
        + [(lambda q: lft_ref[q, 2 * side], x_ref.at[1 - side])]
    )
    residual(parts, mtt_ref[...].astype(F32), res_ref, 1)
    parts = forward(
        [(lambda q, r=r: lfm_ref[side, q, r + 1 - side], x_ref.at[r]) for r in range(2)]
    )
    for n in range(3):
        part_ref[0, n * 128 : (n + 1) * 128, :] = parts[n]
    if not first:
        parts = forward([(lambda q: lff_ref[q, 2 - 2 * side], x_ref.at[side])])
        for n in range(3):
            part_ref[1, n * 128 : (n + 1) * 128, :] = parts[n]
    for p in range(2):
        rows = slice(p * 128, p * 128 + 128)
        for near_far in range(2):
            b = side if near_far else 1 - side
            total = dot(lam_ref[1 - side, b, p], from_residual(res_ref, 0, p))
            for r in range(2):
                total = total + dot(lp_ref[b, p, r + 1 - b], field_of(x_ref.at[r], p))
            if not near_far:
                total = total + dot(lat_ref[p], from_residual(res_ref, 1, p))
                total = total + dot(lp_ref[b, p, 2 - 2 * side], field_of(mate_ref.at[side], p))
            grad_ref[b, rows, :] = total


def finish_kernel(first, *refs):
    if first:
        (side_ref, x_ref, far_ref, mt_ref, lp_ref, lfm_ref, lam_ref, part_ref, grad_ref) = refs[:9]
        sample_ref, noise_hbm = refs[9:11]
        out_ref, compact_ref, lff_ref, laf_ref, mtf_ref = refs[11:16]
        res_ref, sample_buf, noise_buf, sems = refs[16:]
    else:
        (side_ref, far_ref, mt_ref, lp_ref, lfm_ref, lam_ref, part_ref, grad_ref) = refs[:8]
        lff_ref, laf_ref, mtf_ref, sample_ref, noise_hbm = refs[8:13]
        out_ref = refs[13]
        res_ref, out_buf, noise_buf, sems = refs[14:]
    side = side_ref[0]
    coming = [pltpu.make_async_copy(noise_hbm.at[0 if first else 1], noise_buf, sems.at[0])]
    if first:
        coming.append(pltpu.make_async_copy(sample_ref, sample_buf, sems.at[1]))
    for copy in coming:
        copy.start()
    far = [far_ref.at[f * 512 : (f + 1) * 512] for f in range(2)]
    if first:
        weights, meta = unpack_foot(far_ref, 1024)
        mtf_ref[...] = meta.astype(BF)

        def put(q, dr, rows, lanes, value):
            lff_ref[q, dr, rows, lanes] = value

        def put_adjoint(p, rows, value):
            laf_ref[p, rows, :] = value

        build_forward(weights, meta, put)
        build_adjoint(jnp.transpose(weights, (1, 0)), meta, 2 - 2 * side, put_adjoint)
    nearest = far_ref.at[pl.ds(pl.multiple_of((1 - side) * 512, 512), 512)]
    parts = forward([(lambda q: lfm_ref[side, q, 2 * side], nearest)])
    for n in range(3):
        parts[n] = parts[n] + part_ref[0, n * 128 : (n + 1) * 128, :]
    residual(parts, mt_ref[side].astype(F32), res_ref, 0)
    terms = [(lambda q, f=f: lff_ref[q, f + side], far[f]) for f in range(2)]
    if first:
        terms.append((lambda q: lff_ref[q, 2 - 2 * side], x_ref.at[side]))
    parts = forward(terms)
    if not first:
        for n in range(3):
            parts[n] = parts[n] + part_ref[1, n * 128 : (n + 1) * 128, :]
    residual(parts, mtf_ref[...].astype(F32), res_ref, 1)
    for copy in coming:
        copy.wait()
    old_ref = sample_buf if first else sample_ref
    leaving = []
    for near_far in range(2):
        b = side if near_far else 1 - side
        for p in range(2):
            rows = slice(p * 128, p * 128 + 128)
            total = grad_ref[b, rows, :] + dot(lam_ref[side, b, p], from_residual(res_ref, 0, p))
            if near_far:
                total = total + dot(laf_ref[p], from_residual(res_ref, 1, p))
                field = nearest[(1 + 2 * p) * 64 : (5 + 2 * p) * 64, :]
                total = total + dot(lp_ref[b, p, 2 * side], field)
            value = (
                old_ref[b, rows, :]
                - step_size * total
                + math.sqrt(2.0 * step_size) * noise_buf[b, rows, :].astype(F32)
            )
            if first:
                out_ref[b, rows, :] = value
                compact_ref[b, rows, :] = value.astype(BF)
            else:
                out_buf[b, rows, :] = value
                copy = pltpu.make_async_copy(
                    out_buf.at[b, rows], out_ref.at[b, rows], sems.at[1 + 2 * near_far + p]
                )
                copy.start()
                leaving.append(copy)
    for copy in leaving:
        copy.wait()


KIND = BF


def shape(dims, dtype=BF):
    return jax.ShapeDtypeStruct(dims, dtype)


def call(kernel, name, outs, args, spaces, scratch=(), out_space="v", flops=0, moved=0, grant=16):
    kinds = {"v": VM, "s": pltpu.SMEM, "h": pltpu.HBM}
    return pl.pallas_call(
        kernel,
        name=name,
        out_shape=tuple(outs),
        in_specs=[pl.BlockSpec(memory_space=kinds[space]) for space in spaces],
        out_specs=tuple(pl.BlockSpec(memory_space=kinds[out_space]) for _ in outs),
        scratch_shapes=list(scratch),
        compiler_params=pltpu.CompilerParams(vmem_limit_bytes=grant * 1024 * 1024),
        cost_estimate=pl.CostEstimate(flops=flops, bytes_accessed=moved, transcendentals=0),
    )(*args)


def middle_call(first, args):
    outs = []
    if first:
        outs = [
            shape((2, 2, 3, 256, 256)),
            shape((2, 2, 2, 128, 256)),
            shape((2, 3, 256, 256)),
            shape((2, 128, 256)),
            shape((16, 384)),
        ]
    outs += [shape((2, 384, 256), F32), shape((2, 256, 256), F32)]
    return call(
        lambda *refs: middle_kernel(first, *refs),
        "middle_first" if first else "middle_last",
        outs,
        args,
        "s" + "v" * (len(args) - 1),
        scratch=[pltpu.VMEM((2, 512, 256), BF), pltpu.VMEM((2, 384, 256), BF)],
        flops=700000000,
        moved=20000000,
    )


def finish_call(first, args):
    outs = [shape((2, 256, 256), F32)]
    if first:
        outs += [
            shape((2, 256, 256)),
            shape((2, 3, 256, 256)),
            shape((2, 128, 256)),
            shape((16, 384)),
        ]
    spaces = "s" + "v" * (len(args) - 3) + ("hh" if first else "vh")
    return call(
        lambda *refs: finish_kernel(first, *refs),
        "finish_first" if first else "finish_last",
        outs,
        args,
        spaces,
        scratch=[
            pltpu.VMEM((2, 384, 256), BF),
            pltpu.VMEM((2, 256, 256), F32),
            pltpu.VMEM((2, 256, 256), BF),
            pltpu.SemaphoreType.DMA((5,)),
        ],
        out_space="v" if first else "h",
        flops=400000000,
        moved=5000000,
    )


def local(
    sample_field,
    langevin_noise,
    precision,
    pattern,
    foot_weight,
    foot_columns,
    foot_count,
    observed,
    inverse_var,
):
    side = lax.axis_index("lat") % 2
    sides = jnp.full((1,), side, jnp.int32)
    sample = sample_field.reshape(2, 256, 256)
    noise = langevin_noise.reshape(STEPS, 2, 256, 256)
    fw = foot_weight.reshape(2, 256, 256)
    row = jnp.arange(8, dtype=jnp.int32)[:, None]
    stats = jnp.pad(foot_columns.transpose(0, 1, 3, 2), ((0, 0), (0, 0), (0, 4), (0, 0))).astype(F32)
    stats = jnp.where(row == 4, foot_count[:, :, None].astype(F32), stats)
    stats = jnp.where(row == 5, observed[:, :, None], stats)
    stats = jnp.where(row == 6, inverse_var[:, :, None], stats)
    compact, mt, leaving_west, leaving_east = call(
        prepare_kernel,
        "prepare",
        [shape((2, 256, 256)), shape((2, 16, 256)), shape((2, 208, 256)), shape((2, 208, 256))],
        (sample, stats, fw),
        "vvv",
        flops=1000000,
        moved=1000000,
    )
    (lp,) = call(
        prior_matrix_kernel,
        "prior_matrix",
        [shape((2, 2, 3, 128, 256))],
        (pattern, precision),
        "sv",
        scratch=[pltpu.SMEM((72,), jnp.int32)],
        flops=2000000,
        moved=3000000,
    )

    west = shift_lon(leaving_west, 1)
    east = shift_lon(leaving_east, -1)
    middle = jnp.concatenate([west[:, :128], compact, east[:, :128]], axis=1)
    fw = jnp.concatenate([west[:, 128:192], fw, east[:, 128:192]], axis=1)
    mt = jnp.concatenate([west[:, 192:, :64], mt, east[:, 192:, :64]], axis=2)

    def foot_row(row):
        meta = jnp.pad(mt[row], ((0, 0), (0, 128)))
        return jnp.concatenate([fw[row], meta[:, :256], meta[:, 256:]], axis=0)

    foot = jnp.stack([foot_row(0), foot_row(1)])
    far_foot = jnp.where(side == 0, foot[0], foot[1])
    mate_foot = jnp.where(side == 0, foot[1], foot[0])

    def lat_exchange(compact, middle, west, east, far_extra, mate_extra):
        far = swap_lat(jnp.concatenate([middle.reshape(1024, 256)] + far_extra, axis=0), 1)
        halo = jnp.concatenate([west, east], axis=1).reshape(512, 256)
        halo = swap_lat(jnp.concatenate([halo] + mate_extra, axis=0), 0)
        count = lax.axis_size("lat")
        pair = lax.all_gather(
            compact, "lat", axis_index_groups=[[i, i + 1] for i in range(0, count, 2)]
        )
        return far, pair, halo

    far, pair, halo = lat_exchange(
        compact, middle, west[:, :128], east[:, :128], [far_foot], [mate_foot]
    )
    lfm, lam, lft, lat, mtt, part, grad = middle_call(
        True, (sides, middle, fw, mt, pair, halo, lp)
    )
    sample, compact, lff, laf, mtf = finish_call(
        True, (sides, middle, far, mt, lp, lfm, lam, part, grad, sample, noise)
    )

    west = shift_lon(compact[:, 128:], 1)
    east = shift_lon(compact[:, :128], -1)
    middle = jnp.concatenate([west, compact, east], axis=1)
    far, pair, halo = lat_exchange(compact, middle, west, east, [], [])
    part, grad = middle_call(
        False, (sides, middle, mt, pair, halo, lp, lfm, lam, lft, lat, mtt, lff)
    )
    (sample,) = finish_call(
        False, (sides, far, mt, lp, lfm, lam, part, grad, lff, laf, mtf, sample, noise)
    )
    return sample.reshape(sample_field.shape)


def solution(mesh):
    placed = (
        P("lat", "lon", None, None),
        P(None, "lat", "lon", None, None),
        P("lat", "lon", None, None, None),
        P("lat", "lon", None),
        P("lat", "lon", None, None, None),
        P("lat", "lon", None, None),
        P("lat", "lon", None),
        P("lat", "lon", None),
        P("lat", "lon", None),
    )
    return jax.shard_map(
        local, mesh=mesh, in_specs=placed, out_specs=P("lat", "lon", None, None), check_vma=False
    )
```

```python
import math

import jax
import jax.numpy as jnp
from jax import lax
from jax.experimental import pallas as pl
from jax.experimental.pallas import tpu as pltpu
from jax.sharding import PartitionSpec as P

STEPS = 2
step_size = 0.2
BF = jnp.bfloat16
F32 = jnp.float32
VM = pltpu.VMEM


def shift_lon(block, by):
    count = lax.axis_size("lon")
    return lax.ppermute(block, "lon", [(i, (i + by) % count) for i in range(count)])


def swap_lat(block, first):
    count = lax.axis_size("lat")
    pairs = [(i, i + 1) for i in range(first, count - 1, 2)]
    return lax.ppermute(block, "lat", pairs + [(b, a) for a, b in pairs])


def dot(a, b):
    return jnp.dot(a, b, preferred_element_type=F32)


def split(x):
    high = x.astype(BF)
    rest = x - high.astype(F32)
    middle = rest.astype(BF)
    return [high.astype(F32), middle.astype(F32), rest - middle.astype(F32)]


def prepare_kernel(sample_ref, stats_ref, fw_ref, compact_ref, mt_ref, west_ref, east_ref):
    for b in range(2):
        stats = jnp.concatenate([stats_ref[b, c] for c in range(4)], axis=1)
        rows = [stats[0:4]] + split(stats[5:6]) + split(stats[6:7]) + [jnp.zeros((6, 256), F32)]
        meta = jnp.concatenate(rows, axis=0).astype(BF)
        mt_ref[b] = meta
        compact = sample_ref[b].astype(BF)
        compact_ref[b] = compact
        west_ref[b, 0:128, :] = compact[128:256]
        east_ref[b, 0:128, :] = compact[0:128]
        west_ref[b, 128:192, :] = fw_ref[b, 192:256, :]
        east_ref[b, 128:192, :] = fw_ref[b, 0:64, :]
        west_ref[b, 192:208, :] = jnp.concatenate([meta[:, 192:256]] * 4, axis=1)
        east_ref[b, 192:208, :] = meta


def prior_matrix_kernel(pattern_ref, precision_ref, lp_ref, slot_ref):
    for b in range(2):
        for j in range(4):
            for k in range(9):
                slot_ref[(b * 4 + j) * 9 + pattern_ref[b, j, k]] = k
    blank = jnp.zeros((64, 64), BF)
    for b in range(2):
        for p in range(2):
            for dr in range(3):
                for t in range(2):
                    j = 2 * p + t
                    parts = [
                        precision_ref[b, j, slot_ref[(b * 4 + j) * 9 + dr * 3 + o]]
                        for o in range(3)
                    ]
                    parts = [blank] * t + parts + [blank] * (1 - t)
                    lp_ref[b, p, dr, t * 64 : (t + 1) * 64, :] = jnp.concatenate(parts, axis=1)


def lanes_iota(n):
    return lax.broadcasted_iota(jnp.int32, (1, n), 1) // 64


def build_forward(weights, meta, store):
    codes = jnp.transpose(meta, (1, 0))
    for oc in range(6):
        rows = slice(oc * 64, (oc + 1) * 64)
        pair, code = [], []
        for j in range(4):
            one = weights[rows, j * 64 : (j + 1) * 64]
            pair.append(jnp.concatenate([one, one], axis=1).astype(KIND))
            code.append(jnp.broadcast_to(codes[rows, j : j + 1], (64, 128)).astype(KIND))
        for q in range(2):
            at = oc - 2 * q
            if not 0 <= at < 4:
                continue
            for h in range(2):
                shift = 2 * h - at + 2 * q
                col = lanes_iota(128) + shift
                some = any(0 <= shift + x <= 2 for x in range(2))
                for dr in range(3):
                    total = jnp.zeros((64, 128), KIND)
                    if some:
                        need = jnp.where((col >= 0) & (col <= 2), col + 3 * dr, 77)
                        need = jnp.broadcast_to(need.astype(F32), (64, 128)).astype(KIND)
                        for j in range(4):
                            total = jnp.where(code[j] == need, pair[j], total)
                    store(
                        q,
                        dr,
                        slice(at * 64, at * 64 + 64),
                        slice(h * 128, h * 128 + 128),
                        total.astype(BF),
                    )


def build_adjoint(turned, meta, code_row, store):
    for p in range(2):
        lanes = slice(p * 128, p * 128 + 256)
        for t in range(2):
            col = t - lanes_iota(256) + 2
            need = jnp.where((col >= 0) & (col <= 2), col + 3 * code_row, 77).astype(F32)
            total = jnp.zeros((64, 256), F32)
            for j in range(4):
                hit = meta[j : j + 1, lanes] == need
                total = jnp.where(hit, turned[j * 64 : (j + 1) * 64, lanes], total)
            store(p, slice(t * 64, t * 64 + 64), total.astype(BF))


def unpack_foot(foot_ref, at):
    weights = foot_ref[at : at + 384, :].astype(F32)
    meta = [foot_ref[at + 384 : at + 400, :], foot_ref[at + 400 : at + 416, :128]]
    return weights, jnp.concatenate(meta, axis=1).astype(F32)


def forward(terms):
    halves = []
    for q in range(2):
        total = None
        for operand, field in terms:
            term = dot(operand(q), field[q * 256 : (q + 1) * 256, :])
            total = term if total is None else total + term
        halves.append(total)
    low, high = halves
    return [low[:128], low[128:] + high[:128], high[128:]]


def residual(parts, meta, res_ref, slot):
    columns = jnp.transpose(meta, (1, 0))
    obs = columns[:, 4:5] + columns[:, 5:6] + columns[:, 6:7]
    ivar = columns[:, 7:8] + columns[:, 8:9] + columns[:, 9:10]
    for n in range(3):
        rows = slice(n * 128, (n + 1) * 128)
        res_ref[slot, rows, :] = (ivar[rows] * (parts[n] - obs[rows])).astype(BF)


def field_of(x, p):
    return x[(1 + 2 * p) * 64 : (5 + 2 * p) * 64, :]


def from_residual(res_ref, slot, p):
    return res_ref[slot, p * 128 : p * 128 + 256, :]


def middle_kernel(first, *refs):
    if first:
        side_ref, x_ref, fw_ref, mt_ref, pair_ref, halo_ref, lp_ref = refs[:7]
        lfm_ref, lam_ref, lft_ref, lat_ref, mtt_ref, part_ref, grad_ref = refs[7:14]
        mate_ref, res_ref = refs[14:]
    else:
        (side_ref, x_ref, mt_ref, pair_ref, halo_ref, lp_ref) = refs[:6]
        lfm_ref, lam_ref, lft_ref, lat_ref, mtt_ref, lff_ref = refs[6:12]
        part_ref, grad_ref = refs[12:14]
        mate_ref, res_ref = refs[14:]
    side = side_ref[0]
    for m in range(2):
        mate_ref[m, 0:128, :] = halo_ref[1 - side, m * 256 : m * 256 + 128, :]
        mate_ref[m, 128:384, :] = pair_ref[1 - side, m]
        mate_ref[m, 384:512, :] = halo_ref[1 - side, m * 256 + 128 : m * 256 + 256, :]
    if first:
        for k in range(2):
            meta = mt_ref[k].astype(F32)
            weights = fw_ref[k].astype(F32)

            def put(q, dr, rows, lanes, value):
                lfm_ref[k, q, dr, rows, lanes] = value

            build_forward(weights, meta, put)
            turned = jnp.transpose(weights, (1, 0))
            for b in range(2):

                def put_adjoint(p, rows, value):
                    lam_ref[k, b, p, rows, :] = value

                build_adjoint(turned, meta, b - k + 1, put_adjoint)
        weights, meta = unpack_foot(halo_ref.at[1 - side], 512)
        mtt_ref[...] = meta.astype(BF)

        def put_mate(q, dr, rows, lanes, value):
            lft_ref[q, dr, rows, lanes] = value

        def put_mate_adjoint(p, rows, value):
            lat_ref[p, rows, :] = value

        build_forward(weights, meta, put_mate)
        build_adjoint(jnp.transpose(weights, (1, 0)), meta, 2 * side, put_mate_adjoint)

    parts = forward(
        [(lambda q, r=r: lfm_ref[1 - side, q, r + side], x_ref.at[r]) for r in range(2)]
        + [(lambda q: lfm_ref[1 - side, q, 2 - 2 * side], mate_ref.at[side])]
    )
    residual(parts, mt_ref[1 - side].astype(F32), res_ref, 0)
    parts = forward(
        [(lambda q, m=m: lft_ref[q, m + 1 - side], mate_ref.at[m]) for m in range(2)]
        + [(lambda q: lft_ref[q, 2 * side], x_ref.at[1 - side])]
    )
    residual(parts, mtt_ref[...].astype(F32), res_ref, 1)
    parts = forward(
        [(lambda q, r=r: lfm_ref[side, q, r + 1 - side], x_ref.at[r]) for r in range(2)]
    )
    for n in range(3):
        part_ref[0, n * 128 : (n + 1) * 128, :] = parts[n]
    if not first:
        parts = forward([(lambda q: lff_ref[q, 2 - 2 * side], x_ref.at[side])])
        for n in range(3):
            part_ref[1, n * 128 : (n + 1) * 128, :] = parts[n]
    for p in range(2):
        rows = slice(p * 128, p * 128 + 128)
        for near_far in range(2):
            b = side if near_far else 1 - side
            total = dot(lam_ref[1 - side, b, p], from_residual(res_ref, 0, p))
            for r in range(2):
                total = total + dot(lp_ref[b, p, r + 1 - b], field_of(x_ref.at[r], p))
            if not near_far:
                total = total + dot(lat_ref[p], from_residual(res_ref, 1, p))
                total = total + dot(lp_ref[b, p, 2 - 2 * side], field_of(mate_ref.at[side], p))
            grad_ref[b, rows, :] = total


def finish_kernel(first, *refs):
    if first:
        (side_ref, x_ref, own_ref, halo_ref, mt_ref, lp_ref, lfm_ref, lam_ref) = refs[:8]
        part_ref, grad_ref, sample_ref, noise_hbm = refs[8:12]
        out_ref, compact_ref, lff_ref, laf_ref, mtf_ref = refs[12:17]
        res_ref, far_ref, sample_buf, noise_buf, sems = refs[17:]
    else:
        (side_ref, own_ref, halo_ref, mt_ref, lp_ref, lfm_ref, lam_ref, part_ref) = refs[:8]
        grad_ref, lff_ref, laf_ref, mtf_ref, sample_ref, noise_hbm = refs[8:14]
        out_ref = refs[14]
        res_ref, far_ref, out_buf, noise_buf, sems = refs[15:]
    side = side_ref[0]
    coming = [pltpu.make_async_copy(noise_hbm.at[0 if first else 1], noise_buf, sems.at[0])]
    if first:
        coming.append(pltpu.make_async_copy(sample_ref, sample_buf, sems.at[1]))
    for copy in coming:
        copy.start()
    for f in range(2):
        far_ref[f, 0:128, :] = halo_ref[f * 256 : f * 256 + 128, :]
        far_ref[f, 128:384, :] = own_ref[f * 256 : f * 256 + 256, :]
        far_ref[f, 384:512, :] = halo_ref[f * 256 + 128 : f * 256 + 256, :]
    far = [far_ref.at[f] for f in range(2)]
    if first:
        weights = [halo_ref[512:576, :], own_ref[512:768, :], halo_ref[576:640, :]]
        weights = jnp.concatenate(weights, axis=0).astype(F32)
        meta = [halo_ref[640:656, :64], own_ref[768:784, :], halo_ref[640:656, 64:128]]
        meta = jnp.concatenate(meta, axis=1).astype(F32)
        mtf_ref[...] = meta.astype(BF)

        def put(q, dr, rows, lanes, value):
            lff_ref[q, dr, rows, lanes] = value

        def put_adjoint(p, rows, value):
            laf_ref[p, rows, :] = value

        build_forward(weights, meta, put)
        build_adjoint(jnp.transpose(weights, (1, 0)), meta, 2 - 2 * side, put_adjoint)
    nearest = far_ref.at[1 - side]
    parts = forward([(lambda q: lfm_ref[side, q, 2 * side], nearest)])
    for n in range(3):
        parts[n] = parts[n] + part_ref[0, n * 128 : (n + 1) * 128, :]
    residual(parts, mt_ref[side].astype(F32), res_ref, 0)
    terms = [(lambda q, f=f: lff_ref[q, f + side], far[f]) for f in range(2)]
    if first:
        terms.append((lambda q: lff_ref[q, 2 - 2 * side], x_ref.at[side]))
    parts = forward(terms)
    if not first:
        for n in range(3):
            parts[n] = parts[n] + part_ref[1, n * 128 : (n + 1) * 128, :]
    residual(parts, mtf_ref[...].astype(F32), res_ref, 1)
    for copy in coming:
        copy.wait()
    old_ref = sample_buf if first else sample_ref
    leaving = []
    for near_far in range(2):
        b = side if near_far else 1 - side
        for p in range(2):
            rows = slice(p * 128, p * 128 + 128)
            total = grad_ref[b, rows, :] + dot(lam_ref[side, b, p], from_residual(res_ref, 0, p))
            if near_far:
                total = total + dot(laf_ref[p], from_residual(res_ref, 1, p))
                field = nearest[(1 + 2 * p) * 64 : (5 + 2 * p) * 64, :]
                total = total + dot(lp_ref[b, p, 2 * side], field)
            value = (
                old_ref[b, rows, :]
                - step_size * total
                + math.sqrt(2.0 * step_size) * noise_buf[b, rows, :].astype(F32)
            )
            if first:
                out_ref[b, rows, :] = value
                compact_ref[b, rows, :] = value.astype(BF)
            else:
                out_buf[b, rows, :] = value
                copy = pltpu.make_async_copy(
                    out_buf.at[b, rows], out_ref.at[b, rows], sems.at[1 + 2 * near_far + p]
                )
                copy.start()
                leaving.append(copy)
    for copy in leaving:
        copy.wait()


KIND = BF


def shape(dims, dtype=BF):
    return jax.ShapeDtypeStruct(dims, dtype)


def call(kernel, name, outs, args, spaces, scratch=(), out_space="v", flops=0, moved=0, grant=16):
    kinds = {"v": VM, "s": pltpu.SMEM, "h": pltpu.HBM}
    return pl.pallas_call(
        kernel,
        name=name,
        out_shape=tuple(outs),
        in_specs=[pl.BlockSpec(memory_space=kinds[space]) for space in spaces],
        out_specs=tuple(pl.BlockSpec(memory_space=kinds[out_space]) for _ in outs),
        scratch_shapes=list(scratch),
        compiler_params=pltpu.CompilerParams(vmem_limit_bytes=grant * 1024 * 1024),
        cost_estimate=pl.CostEstimate(flops=flops, bytes_accessed=moved, transcendentals=0),
    )(*args)


def middle_call(first, args):
    outs = []
    if first:
        outs = [
            shape((2, 2, 3, 256, 256)),
            shape((2, 2, 2, 128, 256)),
            shape((2, 3, 256, 256)),
            shape((2, 128, 256)),
            shape((16, 384)),
        ]
    outs += [shape((2, 384, 256), F32), shape((2, 256, 256), F32)]
    return call(
        lambda *refs: middle_kernel(first, *refs),
        "middle_first" if first else "middle_last",
        outs,
        args,
        "s" + "v" * (len(args) - 1),
        scratch=[pltpu.VMEM((2, 512, 256), BF), pltpu.VMEM((2, 384, 256), BF)],
        flops=1000000,
        moved=100000,
    )


def finish_call(first, args):
    outs = [shape((2, 256, 256), F32)]
    if first:
        outs += [
            shape((2, 256, 256)),
            shape((2, 3, 256, 256)),
            shape((2, 128, 256)),
            shape((16, 384)),
        ]
    spaces = "s" + "v" * (len(args) - 3) + ("hh" if first else "vh")
    return call(
        lambda *refs: finish_kernel(first, *refs),
        "finish_first" if first else "finish_last",
        outs,
        args,
        spaces,
        scratch=[
            pltpu.VMEM((2, 384, 256), BF),
            pltpu.VMEM((2, 512, 256), BF),
            pltpu.VMEM((2, 256, 256), F32),
            pltpu.VMEM((2, 256, 256), BF),
            pltpu.SemaphoreType.DMA((5,)),
        ],
        out_space="v" if first else "h",
        flops=400000000,
        moved=5000000,
    )


def local(
    sample_field,
    langevin_noise,
    precision,
    pattern,
    foot_weight,
    foot_columns,
    foot_count,
    observed,
    inverse_var,
):
    side = lax.axis_index("lat") % 2
    sides = jnp.full((1,), side, jnp.int32)
    sample = sample_field.reshape(2, 256, 256)
    noise = langevin_noise.reshape(STEPS, 2, 256, 256)
    fw = foot_weight.reshape(2, 256, 256)
    row = jnp.arange(8, dtype=jnp.int32)[:, None]
    codes = jnp.pad(foot_columns.transpose(0, 1, 3, 2), ((0, 0), (0, 0), (0, 4), (0, 0)))
    codes = jnp.where(row < foot_count[:, :, None], codes, 99).astype(F32)
    stats = jnp.where(row == 6, inverse_var[:, :, None], observed[:, :, None])
    stats = jnp.where(row < 4, codes, stats)
    compact, mt, leaving_west, leaving_east = call(
        prepare_kernel,
        "prepare",
        [shape((2, 256, 256)), shape((2, 16, 256)), shape((2, 208, 256)), shape((2, 208, 256))],
        (sample, stats, fw),
        "vvv",
        flops=1000000,
        moved=1000000,
    )
    (lp,) = call(
        prior_matrix_kernel,
        "prior_matrix",
        [shape((2, 2, 3, 128, 256))],
        (pattern, precision),
        "sv",
        scratch=[pltpu.SMEM((72,), jnp.int32)],
        flops=2000000,
        moved=3000000,
    )

    west = shift_lon(leaving_west, 1)
    east = shift_lon(leaving_east, -1)
    fw_own, mt_own = fw, mt

    def near_row(rows):
        return jnp.where(side == 0, rows[0], rows[1])

    own_far = swap_lat(
        jnp.concatenate([compact.reshape(512, 256), near_row(fw_own), near_row(mt_own)], axis=0), 1
    )
    middle = jnp.concatenate([west[:, :128], compact, east[:, :128]], axis=1)
    fw = jnp.concatenate([west[:, 128:192], fw, east[:, 128:192]], axis=1)
    mt = jnp.concatenate([west[:, 192:, :64], mt, east[:, 192:, :64]], axis=2)

    def mates(compact, halo, extra):
        count = lax.axis_size("lat")
        groups = [[i, i + 1] for i in range(0, count, 2)]
        pair = lax.all_gather(compact, "lat", axis_index_groups=groups)
        halo = jnp.concatenate([halo] + extra, axis=0)
        return pair, lax.all_gather(halo, "lat", axis_index_groups=groups)

    halo = jnp.concatenate([west[:, :128], east[:, :128]], axis=1).reshape(512, 256)
    meta = jnp.concatenate([west[:, 192:, :64], east[:, 192:, :64]], axis=2)
    meta = jnp.pad(near_row(meta), ((0, 0), (0, 128)))
    foot = [near_row(west[:, 128:192]), near_row(east[:, 128:192]), meta]
    halo_far = swap_lat(jnp.concatenate([halo] + foot, axis=0), 1)
    mate_meta = jnp.pad(jnp.where(side == 0, mt[1], mt[0]), ((0, 0), (0, 128)))
    mate_foot = [jnp.where(side == 0, fw[1], fw[0]), mate_meta[:, :256], mate_meta[:, 256:]]
    pair, halo = mates(compact, halo, mate_foot)
    lfm, lam, lft, lat, mtt, part, grad = middle_call(
        True, (sides, middle, fw, mt, pair, halo, lp)
    )
    sample, compact, lff, laf, mtf = finish_call(
        True, (sides, middle, own_far, halo_far, mt, lp, lfm, lam, part, grad, sample, noise)
    )

    west = shift_lon(compact[:, 128:], 1)
    east = shift_lon(compact[:, :128], -1)
    own_far = swap_lat(compact.reshape(512, 256), 1)
    middle = jnp.concatenate([west, compact, east], axis=1)
    halo = jnp.concatenate([west, east], axis=1).reshape(512, 256)
    halo_far = swap_lat(halo, 1)
    pair, halo = mates(compact, halo, [])
    part, grad = middle_call(
        False, (sides, middle, mt, pair, halo, lp, lfm, lam, lft, lat, mtt, lff)
    )
    (sample,) = finish_call(
        False, (sides, own_far, halo_far, mt, lp, lfm, lam, part, grad, lff, laf, mtf, sample, noise)
    )
    return sample.reshape(sample_field.shape)


def solution(mesh):
    placed = (
        P("lat", "lon", None, None),
        P(None, "lat", "lon", None, None),
        P("lat", "lon", None, None, None),
        P("lat", "lon", None),
        P("lat", "lon", None, None, None),
        P("lat", "lon", None, None),
        P("lat", "lon", None),
        P("lat", "lon", None),
        P("lat", "lon", None),
    )
    return jax.shard_map(
        local, mesh=mesh, in_specs=placed, out_specs=P("lat", "lon", None, None), check_vma=False
    )
```

```python
import math

import jax
import jax.numpy as jnp
from jax import lax
from jax.experimental import pallas as pl
from jax.experimental.pallas import tpu as pltpu
from jax.sharding import PartitionSpec as P

STEPS = 2
step_size = 0.2
BF = jnp.bfloat16
F32 = jnp.float32
VM = pltpu.VMEM


def shift_lon(block, by):
    count = lax.axis_size("lon")
    return lax.ppermute(block, "lon", [(i, (i + by) % count) for i in range(count)])


def swap_lat(block, first):
    count = lax.axis_size("lat")
    pairs = [(i, i + 1) for i in range(first, count - 1, 2)]
    return lax.ppermute(block, "lat", pairs + [(b, a) for a, b in pairs])


def dot(a, b):
    return jnp.dot(a, b, preferred_element_type=F32)


def split(x):
    high = x.astype(BF)
    rest = x - high.astype(F32)
    middle = rest.astype(BF)
    return [high.astype(F32), middle.astype(F32), rest - middle.astype(F32)]


def prepare_kernel(sample_ref, stats_ref, fw_ref, compact_ref, mt_ref, west_ref, east_ref):
    for b in range(2):
        stats = jnp.concatenate([stats_ref[b, c] for c in range(4)], axis=1)
        rows = [stats[0:4]] + split(stats[5:6]) + split(stats[6:7]) + [jnp.zeros((6, 256), F32)]
        meta = jnp.concatenate(rows, axis=0).astype(BF)
        mt_ref[b] = meta
        compact = sample_ref[b].astype(BF)
        compact_ref[b] = compact
        west_ref[b, 0:128, :] = compact[128:256]
        east_ref[b, 0:128, :] = compact[0:128]
        west_ref[b, 128:192, :] = fw_ref[b, 192:256, :]
        east_ref[b, 128:192, :] = fw_ref[b, 0:64, :]
        west_ref[b, 192:208, :] = jnp.concatenate([meta[:, 192:256]] * 4, axis=1)
        east_ref[b, 192:208, :] = meta


def prior_matrix_kernel(pattern_ref, precision_ref, lp_ref, slot_ref):
    for b in range(2):
        for j in range(4):
            for k in range(9):
                slot_ref[(b * 4 + j) * 9 + pattern_ref[b, j, k]] = k
    blank = jnp.zeros((64, 64), BF)
    for b in range(2):
        for p in range(2):
            for dr in range(3):
                for t in range(2):
                    j = 2 * p + t
                    parts = [
                        precision_ref[b, j, slot_ref[(b * 4 + j) * 9 + dr * 3 + o]]
                        for o in range(3)
                    ]
                    parts = [blank] * t + parts + [blank] * (1 - t)
                    lp_ref[b, p, dr, t * 64 : (t + 1) * 64, :] = jnp.concatenate(parts, axis=1)


def lanes_iota(n):
    return lax.broadcasted_iota(jnp.int32, (1, n), 1) // 64


def build_forward(weights, meta, store):
    codes = jnp.transpose(meta, (1, 0))
    for oc in range(6):
        rows = slice(oc * 64, (oc + 1) * 64)
        pair, code = [], []
        for j in range(4):
            one = weights[rows, j * 64 : (j + 1) * 64]
            pair.append(jnp.concatenate([one, one], axis=1).astype(KIND))
            code.append(jnp.broadcast_to(codes[rows, j : j + 1], (64, 128)).astype(KIND))
        for q in range(2):
            at = oc - 2 * q
            if not 0 <= at < 4:
                continue
            for h in range(2):
                shift = 2 * h - at + 2 * q
                col = lanes_iota(128) + shift
                some = any(0 <= shift + x <= 2 for x in range(2))
                for dr in range(3):
                    total = jnp.zeros((64, 128), KIND)
                    if some:
                        need = jnp.where((col >= 0) & (col <= 2), col + 3 * dr, 77)
                        need = jnp.broadcast_to(need.astype(F32), (64, 128)).astype(KIND)
                        for j in range(4):
                            total = jnp.where(code[j] == need, pair[j], total)
                    store(
                        q,
                        dr,
                        slice(at * 64, at * 64 + 64),
                        slice(h * 128, h * 128 + 128),
                        total.astype(BF),
                    )


def build_adjoint(turned, meta, code_row, store):
    for p in range(2):
        lanes = slice(p * 128, p * 128 + 256)
        for t in range(2):
            col = t - lanes_iota(256) + 2
            need = jnp.where((col >= 0) & (col <= 2), col + 3 * code_row, 77).astype(F32)
            total = jnp.zeros((64, 256), F32)
            for j in range(4):
                hit = meta[j : j + 1, lanes] == need
                total = jnp.where(hit, turned[j * 64 : (j + 1) * 64, lanes], total)
            store(p, slice(t * 64, t * 64 + 64), total.astype(BF))


def unpack_foot(foot_ref, at):
    weights = foot_ref[at : at + 384, :].astype(F32)
    meta = [foot_ref[at + 384 : at + 400, :], foot_ref[at + 400 : at + 416, :128]]
    return weights, jnp.concatenate(meta, axis=1).astype(F32)


def forward(terms):
    halves = []
    for q in range(2):
        total = None
        for operand, field in terms:
            term = dot(operand(q), field[q * 256 : (q + 1) * 256, :])
            total = term if total is None else total + term
        halves.append(total)
    low, high = halves
    return [low[:128], low[128:] + high[:128], high[128:]]


def residual(parts, meta, res_ref, slot):
    columns = jnp.transpose(meta, (1, 0))
    obs = columns[:, 4:5] + columns[:, 5:6] + columns[:, 6:7]
    ivar = columns[:, 7:8] + columns[:, 8:9] + columns[:, 9:10]
    for n in range(3):
        rows = slice(n * 128, (n + 1) * 128)
        res_ref[slot, rows, :] = (ivar[rows] * (parts[n] - obs[rows])).astype(BF)


def field_of(x, p):
    return x[(1 + 2 * p) * 64 : (5 + 2 * p) * 64, :]


def from_residual(res_ref, slot, p):
    return res_ref[slot, p * 128 : p * 128 + 256, :]


def middle_kernel(first, *refs):
    if first:
        side_ref, x_ref, fw_ref, mt_ref, pair_ref, halo_ref, lp_ref = refs[:7]
        lfm_ref, lam_ref, lft_ref, lat_ref, mtt_ref, part_ref, grad_ref = refs[7:14]
        mate_ref, res_ref = refs[14:]
    else:
        (side_ref, x_ref, mt_ref, pair_ref, halo_ref, lp_ref) = refs[:6]
        lfm_ref, lam_ref, lft_ref, lat_ref, mtt_ref, lff_ref = refs[6:12]
        part_ref, grad_ref = refs[12:14]
        mate_ref, res_ref = refs[14:]
    side = side_ref[0]
    for m in range(2):
        mate_ref[m, 0:128, :] = halo_ref[1 - side, m * 256 : m * 256 + 128, :]
        mate_ref[m, 128:384, :] = pair_ref[1 - side, m]
        mate_ref[m, 384:512, :] = halo_ref[1 - side, m * 256 + 128 : m * 256 + 256, :]
    if first:
        for k in range(2):
            meta = mt_ref[k].astype(F32)
            weights = fw_ref[k].astype(F32)

            def put(q, dr, rows, lanes, value):
                lfm_ref[k, q, dr, rows, lanes] = value

            build_forward(weights, meta, put)
            turned = jnp.transpose(weights, (1, 0))
            for b in range(2):

                def put_adjoint(p, rows, value):
                    lam_ref[k, b, p, rows, :] = value

                build_adjoint(turned, meta, b - k + 1, put_adjoint)
        weights, meta = unpack_foot(halo_ref.at[1 - side], 512)
        mtt_ref[...] = meta.astype(BF)

        def put_mate(q, dr, rows, lanes, value):
            lft_ref[q, dr, rows, lanes] = value

        def put_mate_adjoint(p, rows, value):
            lat_ref[p, rows, :] = value

        build_forward(weights, meta, put_mate)
        build_adjoint(jnp.transpose(weights, (1, 0)), meta, 2 * side, put_mate_adjoint)

    parts = forward(
        [(lambda q, r=r: lfm_ref[1 - side, q, r + side], x_ref.at[r]) for r in range(2)]
        + [(lambda q: lfm_ref[1 - side, q, 2 - 2 * side], mate_ref.at[side])]
    )
    residual(parts, mt_ref[1 - side].astype(F32), res_ref, 0)
    parts = forward(
        [(lambda q, m=m: lft_ref[q, m + 1 - side], mate_ref.at[m]) for m in range(2)]
        + [(lambda q: lft_ref[q, 2 * side], x_ref.at[1 - side])]
    )
    residual(parts, mtt_ref[...].astype(F32), res_ref, 1)
    parts = forward(
        [(lambda q, r=r: lfm_ref[side, q, r + 1 - side], x_ref.at[r]) for r in range(2)]
    )
    for n in range(3):
        part_ref[0, n * 128 : (n + 1) * 128, :] = parts[n]
    if not first:
        parts = forward([(lambda q: lff_ref[q, 2 - 2 * side], x_ref.at[side])])
        for n in range(3):
            part_ref[1, n * 128 : (n + 1) * 128, :] = parts[n]
    for p in range(2):
        rows = slice(p * 128, p * 128 + 128)
        for near_far in range(2):
            b = side if near_far else 1 - side
            total = dot(lam_ref[1 - side, b, p], from_residual(res_ref, 0, p))
            for r in range(2):
                total = total + dot(lp_ref[b, p, r + 1 - b], field_of(x_ref.at[r], p))
            if not near_far:
                total = total + dot(lat_ref[p], from_residual(res_ref, 1, p))
                total = total + dot(lp_ref[b, p, 2 - 2 * side], field_of(mate_ref.at[side], p))
            grad_ref[b, rows, :] = total


def finish_kernel(first, *refs):
    if first:
        (side_ref, x_ref, own_ref, halo_ref, mt_ref, lp_ref, lfm_ref, lam_ref) = refs[:8]
        part_ref, grad_ref, sample_ref, noise_hbm = refs[8:12]
        out_ref, compact_ref, lff_ref, laf_ref, mtf_ref = refs[12:17]
        res_ref, far_ref, sample_buf, noise_buf, sems = refs[17:]
    else:
        (side_ref, own_ref, halo_ref, mt_ref, lp_ref, lfm_ref, lam_ref, part_ref) = refs[:8]
        grad_ref, lff_ref, laf_ref, mtf_ref, sample_ref, noise_hbm = refs[8:14]
        out_ref = refs[14]
        res_ref, far_ref, out_buf, noise_buf, sems = refs[15:]
    side = side_ref[0]
    coming = [pltpu.make_async_copy(noise_hbm.at[0 if first else 1], noise_buf, sems.at[0])]
    if first:
        coming.append(pltpu.make_async_copy(sample_ref, sample_buf, sems.at[1]))
    for copy in coming:
        copy.start()
    for f in range(2):
        far_ref[f, 0:128, :] = halo_ref[f * 256 : f * 256 + 128, :]
        far_ref[f, 128:384, :] = own_ref[f * 256 : f * 256 + 256, :]
        far_ref[f, 384:512, :] = halo_ref[f * 256 + 128 : f * 256 + 256, :]
    far = [far_ref.at[f] for f in range(2)]
    if first:
        weights = [halo_ref[512:576, :], own_ref[512:768, :], halo_ref[576:640, :]]
        weights = jnp.concatenate(weights, axis=0).astype(F32)
        meta = [halo_ref[640:656, :64], own_ref[768:784, :], halo_ref[640:656, 64:128]]
        meta = jnp.concatenate(meta, axis=1).astype(F32)
        mtf_ref[...] = meta.astype(BF)

        def put(q, dr, rows, lanes, value):
            lff_ref[q, dr, rows, lanes] = value

        def put_adjoint(p, rows, value):
            laf_ref[p, rows, :] = value

        build_forward(weights, meta, put)
        build_adjoint(jnp.transpose(weights, (1, 0)), meta, 2 - 2 * side, put_adjoint)
    nearest = far_ref.at[1 - side]
    parts = forward([(lambda q: lfm_ref[side, q, 2 * side], nearest)])
    for n in range(3):
        parts[n] = parts[n] + part_ref[0, n * 128 : (n + 1) * 128, :]
    residual(parts, mt_ref[side].astype(F32), res_ref, 0)
    terms = [(lambda q, f=f: lff_ref[q, f + side], far[f]) for f in range(2)]
    if first:
        terms.append((lambda q: lff_ref[q, 2 - 2 * side], x_ref.at[side]))
    parts = forward(terms)
    if not first:
        for n in range(3):
            parts[n] = parts[n] + part_ref[1, n * 128 : (n + 1) * 128, :]
    residual(parts, mtf_ref[...].astype(F32), res_ref, 1)
    for copy in coming:
        copy.wait()
    old_ref = sample_buf if first else sample_ref
    leaving = []
    for near_far in range(2):
        b = side if near_far else 1 - side
        for p in range(2):
            rows = slice(p * 128, p * 128 + 128)
            total = grad_ref[b, rows, :] + dot(lam_ref[side, b, p], from_residual(res_ref, 0, p))
            if near_far:
                total = total + dot(laf_ref[p], from_residual(res_ref, 1, p))
                field = nearest[(1 + 2 * p) * 64 : (5 + 2 * p) * 64, :]
                total = total + dot(lp_ref[b, p, 2 * side], field)
            value = (
                old_ref[b, rows, :]
                - step_size * total
                + math.sqrt(2.0 * step_size) * noise_buf[b, rows, :].astype(F32)
            )
            if first:
                out_ref[b, rows, :] = value
                compact_ref[b, rows, :] = value.astype(BF)
            else:
                out_buf[b, rows, :] = value
                copy = pltpu.make_async_copy(
                    out_buf.at[b, rows], out_ref.at[b, rows], sems.at[1 + 2 * near_far + p]
                )
                copy.start()
                leaving.append(copy)
    for copy in leaving:
        copy.wait()


KIND = BF


def shape(dims, dtype=BF):
    return jax.ShapeDtypeStruct(dims, dtype)


def call(kernel, name, outs, args, spaces, scratch=(), out_space="v", flops=0, moved=0, grant=16):
    kinds = {"v": VM, "s": pltpu.SMEM, "h": pltpu.HBM}
    return pl.pallas_call(
        kernel,
        name=name,
        out_shape=tuple(outs),
        in_specs=[pl.BlockSpec(memory_space=kinds[space]) for space in spaces],
        out_specs=tuple(pl.BlockSpec(memory_space=kinds[out_space]) for _ in outs),
        scratch_shapes=list(scratch),
        compiler_params=pltpu.CompilerParams(vmem_limit_bytes=grant * 1024 * 1024),
        cost_estimate=pl.CostEstimate(flops=flops, bytes_accessed=moved, transcendentals=0),
    )(*args)


def middle_call(first, args):
    outs = []
    if first:
        outs = [
            shape((2, 2, 3, 256, 256)),
            shape((2, 2, 2, 128, 256)),
            shape((2, 3, 256, 256)),
            shape((2, 128, 256)),
            shape((16, 384)),
        ]
    outs += [shape((2, 384, 256), F32), shape((2, 256, 256), F32)]
    return call(
        lambda *refs: middle_kernel(first, *refs),
        "middle_first" if first else "middle_last",
        outs,
        args,
        "s" + "v" * (len(args) - 1),
        scratch=[pltpu.VMEM((2, 512, 256), BF), pltpu.VMEM((2, 384, 256), BF)],
        flops=1000000,
        moved=100000,
    )


def finish_call(first, args):
    outs = [shape((2, 256, 256), F32)]
    if first:
        outs += [
            shape((2, 256, 256)),
            shape((2, 3, 256, 256)),
            shape((2, 128, 256)),
            shape((16, 384)),
        ]
    spaces = "s" + "v" * (len(args) - 3) + ("hh" if first else "vh")
    return call(
        lambda *refs: finish_kernel(first, *refs),
        "finish_first" if first else "finish_last",
        outs,
        args,
        spaces,
        scratch=[
            pltpu.VMEM((2, 384, 256), BF),
            pltpu.VMEM((2, 512, 256), BF),
            pltpu.VMEM((2, 256, 256), F32),
            pltpu.VMEM((2, 256, 256), BF),
            pltpu.SemaphoreType.DMA((5,)),
        ],
        out_space="v" if first else "h",
        flops=400000000,
        moved=5000000,
    )


def local(
    sample_field,
    langevin_noise,
    precision,
    pattern,
    foot_weight,
    foot_columns,
    foot_count,
    observed,
    inverse_var,
):
    side = lax.axis_index("lat") % 2
    sides = jnp.full((1,), side, jnp.int32)
    sample = sample_field.reshape(2, 256, 256)
    noise = langevin_noise.reshape(STEPS, 2, 256, 256)
    fw = foot_weight.reshape(2, 256, 256)
    row = jnp.arange(8, dtype=jnp.int32)[:, None]
    codes = jnp.pad(foot_columns.transpose(0, 1, 3, 2), ((0, 0), (0, 0), (0, 4), (0, 0)))
    codes = jnp.where(row < foot_count[:, :, None], codes, 99).astype(F32)
    stats = jnp.where(row == 6, inverse_var[:, :, None], observed[:, :, None])
    stats = jnp.where(row < 4, codes, stats)
    compact, mt, leaving_west, leaving_east = call(
        prepare_kernel,
        "prepare",
        [shape((2, 256, 256)), shape((2, 16, 256)), shape((2, 208, 256)), shape((2, 208, 256))],
        (sample, stats, fw),
        "vvv",
        flops=1000000,
        moved=1000000,
    )
    west = shift_lon(leaving_west, 1)
    east = shift_lon(leaving_east, -1)
    fw_own, mt_own = fw, mt

    def near_row(rows):
        return jnp.where(side == 0, rows[0], rows[1])

    own_far = swap_lat(
        jnp.concatenate([compact.reshape(512, 256), near_row(fw_own), near_row(mt_own)], axis=0), 1
    )
    middle = jnp.concatenate([west[:, :128], compact, east[:, :128]], axis=1)
    fw = jnp.concatenate([west[:, 128:192], fw, east[:, 128:192]], axis=1)
    mt = jnp.concatenate([west[:, 192:, :64], mt, east[:, 192:, :64]], axis=2)

    def mates(compact, halo, extra):
        count = lax.axis_size("lat")
        groups = [[i, i + 1] for i in range(0, count, 2)]
        pair = lax.all_gather(compact, "lat", axis_index_groups=groups)
        halo = jnp.concatenate([halo] + extra, axis=0)
        return pair, lax.all_gather(halo, "lat", axis_index_groups=groups)

    halo = jnp.concatenate([west[:, :128], east[:, :128]], axis=1).reshape(512, 256)
    mate_own, halo, late_pattern = lax.optimization_barrier((compact, halo, pattern))
    (lp,) = call(
        prior_matrix_kernel,
        "prior_matrix",
        [shape((2, 2, 3, 128, 256))],
        (late_pattern, precision),
        "sv",
        scratch=[pltpu.SMEM((72,), jnp.int32)],
        flops=2000000,
        moved=3000000,
    )
    meta = jnp.concatenate([west[:, 192:, :64], east[:, 192:, :64]], axis=2)
    meta = jnp.pad(near_row(meta), ((0, 0), (0, 128)))
    foot = [near_row(west[:, 128:192]), near_row(east[:, 128:192]), meta]
    halo_far = swap_lat(jnp.concatenate([halo] + foot, axis=0), 1)
    mate_meta = jnp.pad(jnp.where(side == 0, mt[1], mt[0]), ((0, 0), (0, 128)))
    mate_foot = [jnp.where(side == 0, fw[1], fw[0]), mate_meta[:, :256], mate_meta[:, 256:]]
    pair, halo = mates(mate_own, halo, mate_foot)
    lfm, lam, lft, lat, mtt, part, grad = middle_call(
        True, (sides, middle, fw, mt, pair, halo, lp)
    )
    sample, compact, lff, laf, mtf = finish_call(
        True, (sides, middle, own_far, halo_far, mt, lp, lfm, lam, part, grad, sample, noise)
    )

    west = shift_lon(compact[:, 128:], 1)
    east = shift_lon(compact[:, :128], -1)
    own_far = swap_lat(compact.reshape(512, 256), 1)
    middle = jnp.concatenate([west, compact, east], axis=1)
    halo = jnp.concatenate([west, east], axis=1).reshape(512, 256)
    halo_far = swap_lat(halo, 1)
    pair, halo = mates(compact, halo, [])
    part, grad = middle_call(
        False, (sides, middle, mt, pair, halo, lp, lfm, lam, lft, lat, mtt, lff)
    )
    (sample,) = finish_call(
        False, (sides, own_far, halo_far, mt, lp, lfm, lam, part, grad, lff, laf, mtf, sample, noise)
    )
    return sample.reshape(sample_field.shape)


def solution(mesh):
    placed = (
        P("lat", "lon", None, None),
        P(None, "lat", "lon", None, None),
        P("lat", "lon", None, None, None),
        P("lat", "lon", None),
        P("lat", "lon", None, None, None),
        P("lat", "lon", None, None),
        P("lat", "lon", None),
        P("lat", "lon", None),
        P("lat", "lon", None),
    )
    return jax.shard_map(
        local, mesh=mesh, in_specs=placed, out_specs=P("lat", "lon", None, None), check_vma=False
    )
```

```python
import math

import jax
import jax.numpy as jnp
from jax import lax
from jax.experimental import pallas as pl
from jax.experimental.pallas import tpu as pltpu
from jax.sharding import PartitionSpec as P

STEPS = 2
step_size = 0.2
BF = jnp.bfloat16
F32 = jnp.float32
VM = pltpu.VMEM


def shift_lon(block, by):
    count = lax.axis_size("lon")
    return lax.ppermute(block, "lon", [(i, (i + by) % count) for i in range(count)])


def swap_lat(block, first):
    count = lax.axis_size("lat")
    pairs = [(i, i + 1) for i in range(first, count - 1, 2)]
    return lax.ppermute(block, "lat", pairs + [(b, a) for a, b in pairs])


def dot(a, b):
    return jnp.dot(a, b, preferred_element_type=F32)


def split(x):
    high = x.astype(BF)
    rest = x - high.astype(F32)
    middle = rest.astype(BF)
    return [high.astype(F32), middle.astype(F32), rest - middle.astype(F32)]


def prepare_kernel(sample_ref, stats_ref, fw_ref, compact_ref, mt_ref, west_ref, east_ref):
    for b in range(2):
        stats = jnp.concatenate([stats_ref[b, c] for c in range(4)], axis=1)
        rows = [stats[0:4]] + split(stats[5:6]) + split(stats[6:7]) + [jnp.zeros((6, 256), F32)]
        meta = jnp.concatenate(rows, axis=0).astype(BF)
        mt_ref[b] = meta
        compact = sample_ref[b].astype(BF)
        compact_ref[b] = compact
        west_ref[b, 0:128, :] = compact[128:256]
        east_ref[b, 0:128, :] = compact[0:128]
        west_ref[b, 128:192, :] = fw_ref[b, 192:256, :]
        east_ref[b, 128:192, :] = fw_ref[b, 0:64, :]
        west_ref[b, 192:208, :] = jnp.concatenate([meta[:, 192:256]] * 4, axis=1)
        east_ref[b, 192:208, :] = meta


def prior_matrix_kernel(pattern_ref, precision_ref, lp_ref, slot_ref):
    for b in range(2):
        for j in range(4):
            for k in range(9):
                slot_ref[(b * 4 + j) * 9 + pattern_ref[b, j, k]] = k
    blank = jnp.zeros((64, 64), BF)
    for b in range(2):
        for p in range(2):
            for dr in range(3):
                for t in range(2):
                    j = 2 * p + t
                    parts = [
                        precision_ref[b, j, slot_ref[(b * 4 + j) * 9 + dr * 3 + o]]
                        for o in range(3)
                    ]
                    parts = [blank] * t + parts + [blank] * (1 - t)
                    lp_ref[b, p, dr, t * 64 : (t + 1) * 64, :] = jnp.concatenate(parts, axis=1)


def lanes_iota(n):
    return lax.broadcasted_iota(jnp.int32, (1, n), 1) // 64


def build_forward(weights, meta, store):
    codes = jnp.transpose(meta, (1, 0))
    for oc in range(6):
        rows = slice(oc * 64, (oc + 1) * 64)
        pair, code = [], []
        for j in range(4):
            one = weights[rows, j * 64 : (j + 1) * 64]
            pair.append(jnp.concatenate([one, one], axis=1).astype(KIND))
            code.append(jnp.broadcast_to(codes[rows, j : j + 1], (64, 128)).astype(KIND))
        for q in range(2):
            at = oc - 2 * q
            if not 0 <= at < 4:
                continue
            for h in range(2):
                shift = 2 * h - at + 2 * q
                col = lanes_iota(128) + shift
                some = any(0 <= shift + x <= 2 for x in range(2))
                for dr in range(3):
                    total = jnp.zeros((64, 128), KIND)
                    if some:
                        need = jnp.where((col >= 0) & (col <= 2), col + 3 * dr, 77)
                        need = jnp.broadcast_to(need.astype(F32), (64, 128)).astype(KIND)
                        for j in range(4):
                            total = jnp.where(code[j] == need, pair[j], total)
                    store(
                        q,
                        dr,
                        slice(at * 64, at * 64 + 64),
                        slice(h * 128, h * 128 + 128),
                        total.astype(BF),
                    )


def build_adjoint(turned, meta, code_row, store):
    for p in range(2):
        lanes = slice(p * 128, p * 128 + 256)
        for t in range(2):
            col = t - lanes_iota(256) + 2
            need = jnp.where((col >= 0) & (col <= 2), col + 3 * code_row, 77).astype(F32)
            total = jnp.zeros((64, 256), F32)
            for j in range(4):
                hit = meta[j : j + 1, lanes] == need
                total = jnp.where(hit, turned[j * 64 : (j + 1) * 64, lanes], total)
            store(p, slice(t * 64, t * 64 + 64), total.astype(BF))


def unpack_foot(foot_ref, at):
    weights = foot_ref[at : at + 384, :].astype(F32)
    meta = [foot_ref[at + 384 : at + 400, :], foot_ref[at + 400 : at + 416, :128]]
    return weights, jnp.concatenate(meta, axis=1).astype(F32)


def forward(terms):
    halves = []
    for q in range(2):
        total = None
        for operand, field in terms:
            term = dot(operand(q), field[q * 256 : (q + 1) * 256, :])
            total = term if total is None else total + term
        halves.append(total)
    low, high = halves
    return [low[:128], low[128:] + high[:128], high[128:]]


def residual(parts, meta, res_ref, slot):
    columns = jnp.transpose(meta, (1, 0))
    obs = columns[:, 4:5] + columns[:, 5:6] + columns[:, 6:7]
    ivar = columns[:, 7:8] + columns[:, 8:9] + columns[:, 9:10]
    for n in range(3):
        rows = slice(n * 128, (n + 1) * 128)
        res_ref[slot, rows, :] = (ivar[rows] * (parts[n] - obs[rows])).astype(BF)


def field_of(x, p):
    return x[(1 + 2 * p) * 64 : (5 + 2 * p) * 64, :]


def from_residual(res_ref, slot, p):
    return res_ref[slot, p * 128 : p * 128 + 256, :]


def middle_kernel(first, *refs):
    if first:
        side_ref, pattern_ref, x_ref, fw_ref, mt_ref, pair_ref, halo_ref, precision_ref = refs[:8]
        lfm_ref, lam_ref, lft_ref, lat_ref, mtt_ref, part_ref, grad_ref, lp_ref = refs[8:16]
        mate_ref, res_ref, slot_ref = refs[16:]
        prior_matrix_kernel(pattern_ref, precision_ref, lp_ref, slot_ref)
    else:
        (side_ref, x_ref, mt_ref, pair_ref, halo_ref, lp_ref) = refs[:6]
        lfm_ref, lam_ref, lft_ref, lat_ref, mtt_ref, lff_ref = refs[6:12]
        part_ref, grad_ref = refs[12:14]
        mate_ref, res_ref = refs[14:]
    side = side_ref[0]
    for m in range(2):
        mate_ref[m, 0:128, :] = halo_ref[1 - side, m * 256 : m * 256 + 128, :]
        mate_ref[m, 128:384, :] = pair_ref[1 - side, m]
        mate_ref[m, 384:512, :] = halo_ref[1 - side, m * 256 + 128 : m * 256 + 256, :]
    if first:
        for k in range(2):
            meta = mt_ref[k].astype(F32)
            weights = fw_ref[k].astype(F32)

            def put(q, dr, rows, lanes, value):
                lfm_ref[k, q, dr, rows, lanes] = value

            build_forward(weights, meta, put)
            turned = jnp.transpose(weights, (1, 0))
            for b in range(2):

                def put_adjoint(p, rows, value):
                    lam_ref[k, b, p, rows, :] = value

                build_adjoint(turned, meta, b - k + 1, put_adjoint)
        weights, meta = unpack_foot(halo_ref.at[1 - side], 512)
        mtt_ref[...] = meta.astype(BF)

        def put_mate(q, dr, rows, lanes, value):
            lft_ref[q, dr, rows, lanes] = value

        def put_mate_adjoint(p, rows, value):
            lat_ref[p, rows, :] = value

        build_forward(weights, meta, put_mate)
        build_adjoint(jnp.transpose(weights, (1, 0)), meta, 2 * side, put_mate_adjoint)

    parts = forward(
        [(lambda q, r=r: lfm_ref[1 - side, q, r + side], x_ref.at[r]) for r in range(2)]
        + [(lambda q: lfm_ref[1 - side, q, 2 - 2 * side], mate_ref.at[side])]
    )
    residual(parts, mt_ref[1 - side].astype(F32), res_ref, 0)
    parts = forward(
        [(lambda q, m=m: lft_ref[q, m + 1 - side], mate_ref.at[m]) for m in range(2)]
        + [(lambda q: lft_ref[q, 2 * side], x_ref.at[1 - side])]
    )
    residual(parts, mtt_ref[...].astype(F32), res_ref, 1)
    parts = forward(
        [(lambda q, r=r: lfm_ref[side, q, r + 1 - side], x_ref.at[r]) for r in range(2)]
    )
    for n in range(3):
        part_ref[0, n * 128 : (n + 1) * 128, :] = parts[n]
    if not first:
        parts = forward([(lambda q: lff_ref[q, 2 - 2 * side], x_ref.at[side])])
        for n in range(3):
            part_ref[1, n * 128 : (n + 1) * 128, :] = parts[n]
    for p in range(2):
        rows = slice(p * 128, p * 128 + 128)
        for near_far in range(2):
            b = side if near_far else 1 - side
            total = dot(lam_ref[1 - side, b, p], from_residual(res_ref, 0, p))
            for r in range(2):
                total = total + dot(lp_ref[b, p, r + 1 - b], field_of(x_ref.at[r], p))
            if not near_far:
                total = total + dot(lat_ref[p], from_residual(res_ref, 1, p))
                total = total + dot(lp_ref[b, p, 2 - 2 * side], field_of(mate_ref.at[side], p))
            grad_ref[b, rows, :] = total


def finish_kernel(first, *refs):
    if first:
        (side_ref, x_ref, own_ref, halo_ref, mt_ref, lp_ref, lfm_ref, lam_ref) = refs[:8]
        part_ref, grad_ref, sample_ref, noise_hbm = refs[8:12]
        out_ref, compact_ref, lff_ref, laf_ref, mtf_ref = refs[12:17]
        res_ref, far_ref, sample_buf, noise_buf, sems = refs[17:]
    else:
        (side_ref, own_ref, halo_ref, mt_ref, lp_ref, lfm_ref, lam_ref, part_ref) = refs[:8]
        grad_ref, lff_ref, laf_ref, mtf_ref, sample_ref, noise_hbm = refs[8:14]
        out_ref = refs[14]
        res_ref, far_ref, out_buf, noise_buf, sems = refs[15:]
    side = side_ref[0]
    coming = [pltpu.make_async_copy(noise_hbm.at[0 if first else 1], noise_buf, sems.at[0])]
    if first:
        coming.append(pltpu.make_async_copy(sample_ref, sample_buf, sems.at[1]))
    for copy in coming:
        copy.start()
    for f in range(2):
        far_ref[f, 0:128, :] = halo_ref[f * 256 : f * 256 + 128, :]
        far_ref[f, 128:384, :] = own_ref[f * 256 : f * 256 + 256, :]
        far_ref[f, 384:512, :] = halo_ref[f * 256 + 128 : f * 256 + 256, :]
    far = [far_ref.at[f] for f in range(2)]
    if first:
        weights = [halo_ref[512:576, :], own_ref[512:768, :], halo_ref[576:640, :]]
        weights = jnp.concatenate(weights, axis=0).astype(F32)
        meta = [halo_ref[640:656, :64], own_ref[768:784, :], halo_ref[640:656, 64:128]]
        meta = jnp.concatenate(meta, axis=1).astype(F32)
        mtf_ref[...] = meta.astype(BF)

        def put(q, dr, rows, lanes, value):
            lff_ref[q, dr, rows, lanes] = value

        def put_adjoint(p, rows, value):
            laf_ref[p, rows, :] = value

        build_forward(weights, meta, put)
        build_adjoint(jnp.transpose(weights, (1, 0)), meta, 2 - 2 * side, put_adjoint)
    nearest = far_ref.at[1 - side]
    parts = forward([(lambda q: lfm_ref[side, q, 2 * side], nearest)])
    for n in range(3):
        parts[n] = parts[n] + part_ref[0, n * 128 : (n + 1) * 128, :]
    residual(parts, mt_ref[side].astype(F32), res_ref, 0)
    terms = [(lambda q, f=f: lff_ref[q, f + side], far[f]) for f in range(2)]
    if first:
        terms.append((lambda q: lff_ref[q, 2 - 2 * side], x_ref.at[side]))
    parts = forward(terms)
    if not first:
        for n in range(3):
            parts[n] = parts[n] + part_ref[1, n * 128 : (n + 1) * 128, :]
    residual(parts, mtf_ref[...].astype(F32), res_ref, 1)
    for copy in coming:
        copy.wait()
    old_ref = sample_buf if first else sample_ref
    leaving = []
    for near_far in range(2):
        b = side if near_far else 1 - side
        for p in range(2):
            rows = slice(p * 128, p * 128 + 128)
            total = grad_ref[b, rows, :] + dot(lam_ref[side, b, p], from_residual(res_ref, 0, p))
            if near_far:
                total = total + dot(laf_ref[p], from_residual(res_ref, 1, p))
                field = nearest[(1 + 2 * p) * 64 : (5 + 2 * p) * 64, :]
                total = total + dot(lp_ref[b, p, 2 * side], field)
            value = (
                old_ref[b, rows, :]
                - step_size * total
                + math.sqrt(2.0 * step_size) * noise_buf[b, rows, :].astype(F32)
            )
            if first:
                out_ref[b, rows, :] = value
                compact_ref[b, rows, :] = value.astype(BF)
            else:
                out_buf[b, rows, :] = value
                copy = pltpu.make_async_copy(
                    out_buf.at[b, rows], out_ref.at[b, rows], sems.at[1 + 2 * near_far + p]
                )
                copy.start()
                leaving.append(copy)
    for copy in leaving:
        copy.wait()


KIND = BF


def shape(dims, dtype=BF):
    return jax.ShapeDtypeStruct(dims, dtype)


def call(kernel, name, outs, args, spaces, scratch=(), out_space="v", flops=0, moved=0, grant=16):
    kinds = {"v": VM, "s": pltpu.SMEM, "h": pltpu.HBM}
    return pl.pallas_call(
        kernel,
        name=name,
        out_shape=tuple(outs),
        in_specs=[pl.BlockSpec(memory_space=kinds[space]) for space in spaces],
        out_specs=tuple(pl.BlockSpec(memory_space=kinds[out_space]) for _ in outs),
        scratch_shapes=list(scratch),
        compiler_params=pltpu.CompilerParams(vmem_limit_bytes=grant * 1024 * 1024),
        cost_estimate=pl.CostEstimate(flops=flops, bytes_accessed=moved, transcendentals=0),
    )(*args)


def middle_call(first, args):
    outs = []
    if first:
        outs = [
            shape((2, 2, 3, 256, 256)),
            shape((2, 2, 2, 128, 256)),
            shape((2, 3, 256, 256)),
            shape((2, 128, 256)),
            shape((16, 384)),
        ]
    outs += [shape((2, 384, 256), F32), shape((2, 256, 256), F32)]
    outs += [shape((2, 2, 3, 128, 256))] if first else []
    return call(
        lambda *refs: middle_kernel(first, *refs),
        "middle_first" if first else "middle_last",
        outs,
        args,
        ("ss" if first else "s") + "v" * (len(args) - (2 if first else 1)),
        scratch=[pltpu.VMEM((2, 512, 256), BF), pltpu.VMEM((2, 384, 256), BF)]
        + ([pltpu.SMEM((72,), jnp.int32)] if first else []),
        flops=1000000,
        moved=100000,
    )


def finish_call(first, args):
    outs = [shape((2, 256, 256), F32)]
    if first:
        outs += [
            shape((2, 256, 256)),
            shape((2, 3, 256, 256)),
            shape((2, 128, 256)),
            shape((16, 384)),
        ]
    spaces = "s" + "v" * (len(args) - 3) + ("hh" if first else "vh")
    return call(
        lambda *refs: finish_kernel(first, *refs),
        "finish_first" if first else "finish_last",
        outs,
        args,
        spaces,
        scratch=[
            pltpu.VMEM((2, 384, 256), BF),
            pltpu.VMEM((2, 512, 256), BF),
            pltpu.VMEM((2, 256, 256), F32),
            pltpu.VMEM((2, 256, 256), BF),
            pltpu.SemaphoreType.DMA((5,)),
        ],
        out_space="v" if first else "h",
        flops=400000000,
        moved=5000000,
    )


def local(
    sample_field,
    langevin_noise,
    precision,
    pattern,
    foot_weight,
    foot_columns,
    foot_count,
    observed,
    inverse_var,
):
    side = lax.axis_index("lat") % 2
    sides = jnp.full((1,), side, jnp.int32)
    sample = sample_field.reshape(2, 256, 256)
    noise = langevin_noise.reshape(STEPS, 2, 256, 256)
    fw = foot_weight.reshape(2, 256, 256)
    row = jnp.arange(8, dtype=jnp.int32)[:, None]
    codes = jnp.pad(foot_columns.transpose(0, 1, 3, 2), ((0, 0), (0, 0), (0, 4), (0, 0)))
    codes = jnp.where(row < foot_count[:, :, None], codes, 99).astype(F32)
    stats = jnp.where(row == 6, inverse_var[:, :, None], observed[:, :, None])
    stats = jnp.where(row < 4, codes, stats)
    compact, mt, leaving_west, leaving_east = call(
        prepare_kernel,
        "prepare",
        [shape((2, 256, 256)), shape((2, 16, 256)), shape((2, 208, 256)), shape((2, 208, 256))],
        (sample, stats, fw),
        "vvv",
        flops=1000000,
        moved=1000000,
    )
    west = shift_lon(leaving_west, 1)
    east = shift_lon(leaving_east, -1)
    fw_own, mt_own = fw, mt

    def near_row(rows):
        return jnp.where(side == 0, rows[0], rows[1])

    own_far = swap_lat(
        jnp.concatenate([compact.reshape(512, 256), near_row(fw_own), near_row(mt_own)], axis=0), 1
    )
    middle = jnp.concatenate([west[:, :128], compact, east[:, :128]], axis=1)
    fw = jnp.concatenate([west[:, 128:192], fw, east[:, 128:192]], axis=1)
    mt = jnp.concatenate([west[:, 192:, :64], mt, east[:, 192:, :64]], axis=2)

    def mates(compact, halo, extra):
        count = lax.axis_size("lat")
        groups = [[i, i + 1] for i in range(0, count, 2)]
        pair = lax.all_gather(compact, "lat", axis_index_groups=groups)
        halo = jnp.concatenate([halo] + extra, axis=0)
        return pair, lax.all_gather(halo, "lat", axis_index_groups=groups)

    halo = jnp.concatenate([west[:, :128], east[:, :128]], axis=1).reshape(512, 256)
    mate_own, halo = lax.optimization_barrier((compact, halo))
    meta = jnp.concatenate([west[:, 192:, :64], east[:, 192:, :64]], axis=2)
    meta = jnp.pad(near_row(meta), ((0, 0), (0, 128)))
    foot = [near_row(west[:, 128:192]), near_row(east[:, 128:192]), meta]
    halo_far = swap_lat(jnp.concatenate([halo] + foot, axis=0), 1)
    mate_meta = jnp.pad(jnp.where(side == 0, mt[1], mt[0]), ((0, 0), (0, 128)))
    mate_foot = [jnp.where(side == 0, fw[1], fw[0]), mate_meta[:, :256], mate_meta[:, 256:]]
    pair, halo = mates(mate_own, halo, mate_foot)
    lfm, lam, lft, lat, mtt, part, grad, lp = middle_call(
        True, (sides, pattern, middle, fw, mt, pair, halo, precision)
    )
    sample, compact, lff, laf, mtf = finish_call(
        True, (sides, middle, own_far, halo_far, mt, lp, lfm, lam, part, grad, sample, noise)
    )

    west = shift_lon(compact[:, 128:], 1)
    east = shift_lon(compact[:, :128], -1)
    own_far = swap_lat(compact.reshape(512, 256), 1)
    middle = jnp.concatenate([west, compact, east], axis=1)
    halo = jnp.concatenate([west, east], axis=1).reshape(512, 256)
    halo_far = swap_lat(halo, 1)
    pair, halo = mates(compact, halo, [])
    part, grad = middle_call(
        False, (sides, middle, mt, pair, halo, lp, lfm, lam, lft, lat, mtt, lff)
    )
    (sample,) = finish_call(
        False, (sides, own_far, halo_far, mt, lp, lfm, lam, part, grad, lff, laf, mtf, sample, noise)
    )
    return sample.reshape(sample_field.shape)


def solution(mesh):
    placed = (
        P("lat", "lon", None, None),
        P(None, "lat", "lon", None, None),
        P("lat", "lon", None, None, None),
        P("lat", "lon", None),
        P("lat", "lon", None, None, None),
        P("lat", "lon", None, None),
        P("lat", "lon", None),
        P("lat", "lon", None),
        P("lat", "lon", None),
    )
    return jax.shard_map(
        local, mesh=mesh, in_specs=placed, out_specs=P("lat", "lon", None, None), check_vma=False
    )
```

```python
import math

import jax
import jax.numpy as jnp
from jax import lax
from jax.experimental import pallas as pl
from jax.experimental.pallas import tpu as pltpu
from jax.sharding import PartitionSpec as P

STEPS = 2
step_size = 0.2
BF = jnp.bfloat16
F32 = jnp.float32
VM = pltpu.VMEM


def shift_lon(block, by):
    count = lax.axis_size("lon")
    return lax.ppermute(block, "lon", [(i, (i + by) % count) for i in range(count)])


def swap_lat(block, first):
    count = lax.axis_size("lat")
    pairs = [(i, i + 1) for i in range(first, count - 1, 2)]
    return lax.ppermute(block, "lat", pairs + [(b, a) for a, b in pairs])


def dot(a, b):
    return jnp.dot(a, b, preferred_element_type=F32)


def split(x):
    high = x.astype(BF)
    rest = x - high.astype(F32)
    middle = rest.astype(BF)
    return [high.astype(F32), middle.astype(F32), rest - middle.astype(F32)]


def prepare_kernel(sample_ref, stats_ref, fw_ref, compact_ref, mt_ref, west_ref, east_ref):
    for b in range(2):
        stats = jnp.concatenate([stats_ref[b, c] for c in range(4)], axis=1)
        rows = [stats[0:4]] + split(stats[5:6]) + split(stats[6:7]) + [jnp.zeros((6, 256), F32)]
        meta = jnp.concatenate(rows, axis=0).astype(BF)
        mt_ref[b] = meta
        compact = sample_ref[b].astype(BF)
        compact_ref[b] = compact
        west_ref[b, 0:128, :] = compact[128:256]
        east_ref[b, 0:128, :] = compact[0:128]
        west_ref[b, 128:192, :] = fw_ref[b, 192:256, :]
        east_ref[b, 128:192, :] = fw_ref[b, 0:64, :]
        west_ref[b, 192:208, :] = jnp.concatenate([meta[:, 192:256]] * 4, axis=1)
        east_ref[b, 192:208, :] = meta


def prior_matrix_kernel(pattern_ref, precision_ref, lp_ref, slot_ref):
    for b in range(2):
        for j in range(4):
            for k in range(9):
                slot_ref[(b * 4 + j) * 9 + pattern_ref[b, j, k]] = k
    blank = jnp.zeros((64, 64), BF)
    for b in range(2):
        for p in range(2):
            for dr in range(3):
                for t in range(2):
                    j = 2 * p + t
                    parts = [
                        precision_ref[b, j, slot_ref[(b * 4 + j) * 9 + dr * 3 + o]]
                        for o in range(3)
                    ]
                    parts = [blank] * t + parts + [blank] * (1 - t)
                    lp_ref[b, p, dr, t * 64 : (t + 1) * 64, :] = jnp.concatenate(parts, axis=1)


def lanes_iota(n):
    return lax.broadcasted_iota(jnp.int32, (1, n), 1) // 64


def build_forward(weights, meta, store, owners=range(6)):
    codes = jnp.transpose(meta, (1, 0))
    for oc in owners:
        rows = slice(oc * 64, (oc + 1) * 64)
        pair, code = [], []
        for j in range(4):
            one = weights[rows, j * 64 : (j + 1) * 64]
            pair.append(jnp.concatenate([one, one], axis=1).astype(KIND))
            code.append(jnp.broadcast_to(codes[rows, j : j + 1], (64, 128)).astype(KIND))
        for q in range(2):
            at = oc - 2 * q
            if not 0 <= at < 4:
                continue
            for h in range(2):
                shift = 2 * h - at + 2 * q
                col = lanes_iota(128) + shift
                some = any(0 <= shift + x <= 2 for x in range(2))
                for dr in range(3):
                    total = jnp.zeros((64, 128), KIND)
                    if some:
                        need = jnp.where((col >= 0) & (col <= 2), col + 3 * dr, 77)
                        need = jnp.broadcast_to(need.astype(F32), (64, 128)).astype(KIND)
                        for j in range(4):
                            total = jnp.where(code[j] == need, pair[j], total)
                    store(
                        q,
                        dr,
                        slice(at * 64, at * 64 + 64),
                        slice(h * 128, h * 128 + 128),
                        total.astype(BF),
                    )


def build_adjoint(turned, meta, code_row, store):
    for p in range(2):
        lanes = slice(p * 128, p * 128 + 256)
        for t in range(2):
            col = t - lanes_iota(256) + 2
            need = jnp.where((col >= 0) & (col <= 2), col + 3 * code_row, 77).astype(F32)
            total = jnp.zeros((64, 256), F32)
            for j in range(4):
                hit = meta[j : j + 1, lanes] == need
                total = jnp.where(hit, turned[j * 64 : (j + 1) * 64, lanes], total)
            store(p, slice(t * 64, t * 64 + 64), total.astype(BF))


def unpack_foot(foot_ref, at):
    weights = foot_ref[at : at + 384, :].astype(F32)
    meta = [foot_ref[at + 384 : at + 400, :], foot_ref[at + 400 : at + 416, :128]]
    return weights, jnp.concatenate(meta, axis=1).astype(F32)


def forward(terms):
    halves = []
    for q in range(2):
        total = None
        for operand, field in terms:
            term = dot(operand(q), field[q * 256 : (q + 1) * 256, :])
            total = term if total is None else total + term
        halves.append(total)
    low, high = halves
    return [low[:128], low[128:] + high[:128], high[128:]]


def residual(parts, meta, res_ref, slot):
    columns = jnp.transpose(meta, (1, 0))
    obs = columns[:, 4:5] + columns[:, 5:6] + columns[:, 6:7]
    ivar = columns[:, 7:8] + columns[:, 8:9] + columns[:, 9:10]
    for n in range(3):
        rows = slice(n * 128, (n + 1) * 128)
        res_ref[slot, rows, :] = (ivar[rows] * (parts[n] - obs[rows])).astype(BF)


def field_of(x, p):
    return x[(1 + 2 * p) * 64 : (5 + 2 * p) * 64, :]


def from_residual(res_ref, slot, p):
    return res_ref[slot, p * 128 : p * 128 + 256, :]


def middle_kernel(first, *refs):
    if first:
        side_ref, pattern_ref, x_ref, fw_ref, mt_ref, pair_ref, halo_ref, precision_ref = refs[:8]
        far_ref = refs[8]
        lfm_ref, lam_ref, lft_ref, lat_ref, mtt_ref, part_ref, grad_ref, lp_ref = refs[9:17]
        early_ref = refs[17]
        mate_ref, res_ref, slot_ref = refs[18:]
        prior_matrix_kernel(pattern_ref, precision_ref, lp_ref, slot_ref)
    else:
        (side_ref, x_ref, mt_ref, pair_ref, halo_ref, lp_ref) = refs[:6]
        lfm_ref, lam_ref, lft_ref, lat_ref, mtt_ref, lff_ref = refs[6:12]
        part_ref, grad_ref = refs[12:14]
        mate_ref, res_ref = refs[14:]
    side = side_ref[0]
    for m in range(2):
        mate_ref[m, 0:128, :] = halo_ref[1 - side, m * 256 : m * 256 + 128, :]
        mate_ref[m, 128:384, :] = pair_ref[1 - side, m]
        mate_ref[m, 384:512, :] = halo_ref[1 - side, m * 256 + 128 : m * 256 + 256, :]
    if first:
        for k in range(2):
            meta = mt_ref[k].astype(F32)
            weights = fw_ref[k].astype(F32)

            def put(q, dr, rows, lanes, value):
                lfm_ref[k, q, dr, rows, lanes] = value

            build_forward(weights, meta, put)
            turned = jnp.transpose(weights, (1, 0))
            for b in range(2):

                def put_adjoint(p, rows, value):
                    lam_ref[k, b, p, rows, :] = value

                build_adjoint(turned, meta, b - k + 1, put_adjoint)
        weights, meta = unpack_foot(halo_ref.at[1 - side], 512)
        mtt_ref[...] = meta.astype(BF)

        def put_mate(q, dr, rows, lanes, value):
            lft_ref[q, dr, rows, lanes] = value

        def put_mate_adjoint(p, rows, value):
            lat_ref[p, rows, :] = value

        build_forward(weights, meta, put_mate)

        def put_early(q, dr, rows, lanes, value):
            early_ref[q, dr, rows, lanes] = value

        blank, edge = jnp.zeros((64, 256), F32), jnp.zeros((16, 64), F32)
        far_weights = [blank, far_ref[512:768, :].astype(F32), blank]
        far_meta = [edge, far_ref[768:784, :].astype(F32), edge]
        build_forward(
            jnp.concatenate(far_weights, axis=0),
            jnp.concatenate(far_meta, axis=1),
            put_early,
            range(1, 5),
        )
        build_adjoint(jnp.transpose(weights, (1, 0)), meta, 2 * side, put_mate_adjoint)

    parts = forward(
        [(lambda q, r=r: lfm_ref[1 - side, q, r + side], x_ref.at[r]) for r in range(2)]
        + [(lambda q: lfm_ref[1 - side, q, 2 - 2 * side], mate_ref.at[side])]
    )
    residual(parts, mt_ref[1 - side].astype(F32), res_ref, 0)
    parts = forward(
        [(lambda q, m=m: lft_ref[q, m + 1 - side], mate_ref.at[m]) for m in range(2)]
        + [(lambda q: lft_ref[q, 2 * side], x_ref.at[1 - side])]
    )
    residual(parts, mtt_ref[...].astype(F32), res_ref, 1)
    parts = forward(
        [(lambda q, r=r: lfm_ref[side, q, r + 1 - side], x_ref.at[r]) for r in range(2)]
    )
    for n in range(3):
        part_ref[0, n * 128 : (n + 1) * 128, :] = parts[n]
    if not first:
        parts = forward([(lambda q: lff_ref[q, 2 - 2 * side], x_ref.at[side])])
        for n in range(3):
            part_ref[1, n * 128 : (n + 1) * 128, :] = parts[n]
    for p in range(2):
        rows = slice(p * 128, p * 128 + 128)
        for near_far in range(2):
            b = side if near_far else 1 - side
            total = dot(lam_ref[1 - side, b, p], from_residual(res_ref, 0, p))
            for r in range(2):
                total = total + dot(lp_ref[b, p, r + 1 - b], field_of(x_ref.at[r], p))
            if not near_far:
                total = total + dot(lat_ref[p], from_residual(res_ref, 1, p))
                total = total + dot(lp_ref[b, p, 2 - 2 * side], field_of(mate_ref.at[side], p))
            grad_ref[b, rows, :] = total


def finish_kernel(first, *refs):
    if first:
        (side_ref, x_ref, own_ref, halo_ref, mt_ref, lp_ref, lfm_ref, lam_ref) = refs[:8]
        part_ref, grad_ref, early_ref, sample_ref, noise_hbm = refs[8:13]
        out_ref, compact_ref, lff_ref, laf_ref, mtf_ref = refs[13:18]
        res_ref, far_ref, sample_buf, noise_buf, sems = refs[18:]
    else:
        (side_ref, own_ref, halo_ref, mt_ref, lp_ref, lfm_ref, lam_ref, part_ref) = refs[:8]
        grad_ref, lff_ref, laf_ref, mtf_ref, sample_ref, noise_hbm = refs[8:14]
        out_ref = refs[14]
        res_ref, far_ref, out_buf, noise_buf, sems = refs[15:]
    side = side_ref[0]
    coming = [pltpu.make_async_copy(noise_hbm.at[0 if first else 1], noise_buf, sems.at[0])]
    if first:
        coming.append(pltpu.make_async_copy(sample_ref, sample_buf, sems.at[1]))
    for copy in coming:
        copy.start()
    for f in range(2):
        far_ref[f, 0:128, :] = halo_ref[f * 256 : f * 256 + 128, :]
        far_ref[f, 128:384, :] = own_ref[f * 256 : f * 256 + 256, :]
        far_ref[f, 384:512, :] = halo_ref[f * 256 + 128 : f * 256 + 256, :]
    far = [far_ref.at[f] for f in range(2)]
    if first:
        weights = [halo_ref[512:576, :], own_ref[512:768, :], halo_ref[576:640, :]]
        weights = jnp.concatenate(weights, axis=0).astype(F32)
        meta = [halo_ref[640:656, :64], own_ref[768:784, :], halo_ref[640:656, 64:128]]
        meta = jnp.concatenate(meta, axis=1).astype(F32)
        mtf_ref[...] = meta.astype(BF)

        def put(q, dr, rows, lanes, value):
            lff_ref[q, dr, rows, lanes] = value

        def put_adjoint(p, rows, value):
            laf_ref[p, rows, :] = value

        lff_ref[0, :, 64:256, :] = early_ref[0, :, 64:256, :]
        lff_ref[1, :, 0:192, :] = early_ref[1, :, 0:192, :]
        build_forward(weights, meta, put, (0, 5))
        build_adjoint(jnp.transpose(weights, (1, 0)), meta, 2 - 2 * side, put_adjoint)
    nearest = far_ref.at[1 - side]
    parts = forward([(lambda q: lfm_ref[side, q, 2 * side], nearest)])
    for n in range(3):
        parts[n] = parts[n] + part_ref[0, n * 128 : (n + 1) * 128, :]
    residual(parts, mt_ref[side].astype(F32), res_ref, 0)
    terms = [(lambda q, f=f: lff_ref[q, f + side], far[f]) for f in range(2)]
    if first:
        terms.append((lambda q: lff_ref[q, 2 - 2 * side], x_ref.at[side]))
    parts = forward(terms)
    if not first:
        for n in range(3):
            parts[n] = parts[n] + part_ref[1, n * 128 : (n + 1) * 128, :]
    residual(parts, mtf_ref[...].astype(F32), res_ref, 1)
    for copy in coming:
        copy.wait()
    old_ref = sample_buf if first else sample_ref
    leaving = []
    for near_far in range(2):
        b = side if near_far else 1 - side
        for p in range(2):
            rows = slice(p * 128, p * 128 + 128)
            total = grad_ref[b, rows, :] + dot(lam_ref[side, b, p], from_residual(res_ref, 0, p))
            if near_far:
                total = total + dot(laf_ref[p], from_residual(res_ref, 1, p))
                field = nearest[(1 + 2 * p) * 64 : (5 + 2 * p) * 64, :]
                total = total + dot(lp_ref[b, p, 2 * side], field)
            value = (
                old_ref[b, rows, :]
                - step_size * total
                + math.sqrt(2.0 * step_size) * noise_buf[b, rows, :].astype(F32)
            )
            if first:
                out_ref[b, rows, :] = value
                compact_ref[b, rows, :] = value.astype(BF)
            else:
                out_buf[b, rows, :] = value
                copy = pltpu.make_async_copy(
                    out_buf.at[b, rows], out_ref.at[b, rows], sems.at[1 + 2 * near_far + p]
                )
                copy.start()
                leaving.append(copy)
    for copy in leaving:
        copy.wait()


KIND = BF


def shape(dims, dtype=BF):
    return jax.ShapeDtypeStruct(dims, dtype)


def call(kernel, name, outs, args, spaces, scratch=(), out_space="v", flops=0, moved=0, grant=16):
    kinds = {"v": VM, "s": pltpu.SMEM, "h": pltpu.HBM}
    return pl.pallas_call(
        kernel,
        name=name,
        out_shape=tuple(outs),
        in_specs=[pl.BlockSpec(memory_space=kinds[space]) for space in spaces],
        out_specs=tuple(pl.BlockSpec(memory_space=kinds[out_space]) for _ in outs),
        scratch_shapes=list(scratch),
        compiler_params=pltpu.CompilerParams(vmem_limit_bytes=grant * 1024 * 1024),
        cost_estimate=pl.CostEstimate(flops=flops, bytes_accessed=moved, transcendentals=0),
    )(*args)


def middle_call(first, args):
    outs = []
    if first:
        outs = [
            shape((2, 2, 3, 256, 256)),
            shape((2, 2, 2, 128, 256)),
            shape((2, 3, 256, 256)),
            shape((2, 128, 256)),
            shape((16, 384)),
        ]
    outs += [shape((2, 384, 256), F32), shape((2, 256, 256), F32)]
    outs += [shape((2, 2, 3, 128, 256)), shape((2, 3, 256, 256))] if first else []
    return call(
        lambda *refs: middle_kernel(first, *refs),
        "middle_first" if first else "middle_last",
        outs,
        args,
        ("ss" if first else "s") + "v" * (len(args) - (2 if first else 1)),
        scratch=[pltpu.VMEM((2, 512, 256), BF), pltpu.VMEM((2, 384, 256), BF)]
        + ([pltpu.SMEM((72,), jnp.int32)] if first else []),
        flops=1000000,
        moved=100000,
    )


def finish_call(first, args):
    outs = [shape((2, 256, 256), F32)]
    if first:
        outs += [
            shape((2, 256, 256)),
            shape((2, 3, 256, 256)),
            shape((2, 128, 256)),
            shape((16, 384)),
        ]
    spaces = "s" + "v" * (len(args) - 3) + ("hh" if first else "vh")
    return call(
        lambda *refs: finish_kernel(first, *refs),
        "finish_first" if first else "finish_last",
        outs,
        args,
        spaces,
        scratch=[
            pltpu.VMEM((2, 384, 256), BF),
            pltpu.VMEM((2, 512, 256), BF),
            pltpu.VMEM((2, 256, 256), F32),
            pltpu.VMEM((2, 256, 256), BF),
            pltpu.SemaphoreType.DMA((5,)),
        ],
        out_space="v" if first else "h",
        flops=400000000,
        moved=5000000,
    )


def local(
    sample_field,
    langevin_noise,
    precision,
    pattern,
    foot_weight,
    foot_columns,
    foot_count,
    observed,
    inverse_var,
):
    side = lax.axis_index("lat") % 2
    sides = jnp.full((1,), side, jnp.int32)
    sample = sample_field.reshape(2, 256, 256)
    noise = langevin_noise.reshape(STEPS, 2, 256, 256)
    fw = foot_weight.reshape(2, 256, 256)
    row = jnp.arange(8, dtype=jnp.int32)[:, None]
    codes = jnp.pad(foot_columns.transpose(0, 1, 3, 2), ((0, 0), (0, 0), (0, 4), (0, 0)))
    codes = jnp.where(row < foot_count[:, :, None], codes, 99).astype(F32)
    stats = jnp.where(row == 6, inverse_var[:, :, None], observed[:, :, None])
    stats = jnp.where(row < 4, codes, stats)
    compact, mt, leaving_west, leaving_east = call(
        prepare_kernel,
        "prepare",
        [shape((2, 256, 256)), shape((2, 16, 256)), shape((2, 208, 256)), shape((2, 208, 256))],
        (sample, stats, fw),
        "vvv",
        flops=1000000,
        moved=1000000,
    )
    west = shift_lon(leaving_west, 1)
    east = shift_lon(leaving_east, -1)
    fw_own, mt_own = fw, mt

    def near_row(rows):
        return jnp.where(side == 0, rows[0], rows[1])

    own_far = swap_lat(
        jnp.concatenate([compact.reshape(512, 256), near_row(fw_own), near_row(mt_own)], axis=0), 1
    )
    middle = jnp.concatenate([west[:, :128], compact, east[:, :128]], axis=1)
    fw = jnp.concatenate([west[:, 128:192], fw, east[:, 128:192]], axis=1)
    mt = jnp.concatenate([west[:, 192:, :64], mt, east[:, 192:, :64]], axis=2)

    def mates(compact, halo, extra):
        count = lax.axis_size("lat")
        groups = [[i, i + 1] for i in range(0, count, 2)]
        pair = lax.all_gather(compact, "lat", axis_index_groups=groups)
        halo = jnp.concatenate([halo] + extra, axis=0)
        return pair, lax.all_gather(halo, "lat", axis_index_groups=groups)

    halo = jnp.concatenate([west[:, :128], east[:, :128]], axis=1).reshape(512, 256)
    mate_own, halo = lax.optimization_barrier((compact, halo))
    meta = jnp.concatenate([west[:, 192:, :64], east[:, 192:, :64]], axis=2)
    meta = jnp.pad(near_row(meta), ((0, 0), (0, 128)))
    foot = [near_row(west[:, 128:192]), near_row(east[:, 128:192]), meta]
    halo_far = swap_lat(jnp.concatenate([halo] + foot, axis=0), 1)
    mate_meta = jnp.pad(jnp.where(side == 0, mt[1], mt[0]), ((0, 0), (0, 128)))
    mate_foot = [jnp.where(side == 0, fw[1], fw[0]), mate_meta[:, :256], mate_meta[:, 256:]]
    pair, halo = mates(mate_own, halo, mate_foot)
    lfm, lam, lft, lat, mtt, part, grad, lp, early = middle_call(
        True, (sides, pattern, middle, fw, mt, pair, halo, precision, own_far)
    )
    sample, compact, lff, laf, mtf = finish_call(
        True, (sides, middle, own_far, halo_far, mt, lp, lfm, lam, part, grad, early, sample, noise)
    )

    west = shift_lon(compact[:, 128:], 1)
    east = shift_lon(compact[:, :128], -1)
    own_far = swap_lat(compact.reshape(512, 256), 1)
    middle = jnp.concatenate([west, compact, east], axis=1)
    halo = jnp.concatenate([west, east], axis=1).reshape(512, 256)
    halo_far = swap_lat(halo, 1)
    pair, halo = mates(compact, halo, [])
    part, grad = middle_call(
        False, (sides, middle, mt, pair, halo, lp, lfm, lam, lft, lat, mtt, lff)
    )
    (sample,) = finish_call(
        False, (sides, own_far, halo_far, mt, lp, lfm, lam, part, grad, lff, laf, mtf, sample, noise)
    )
    return sample.reshape(sample_field.shape)


def solution(mesh):
    placed = (
        P("lat", "lon", None, None),
        P(None, "lat", "lon", None, None),
        P("lat", "lon", None, None, None),
        P("lat", "lon", None),
        P("lat", "lon", None, None, None),
        P("lat", "lon", None, None),
        P("lat", "lon", None),
        P("lat", "lon", None),
        P("lat", "lon", None),
    )
    return jax.shard_map(
        local, mesh=mesh, in_specs=placed, out_specs=P("lat", "lon", None, None), check_vma=False
    )
```
